32 devices in a mesh: row: 4 (over z), col: 8 (over y, x, core).
Axes of the slice: x: 2, y: 2, z: 4, core: 2. Of those that a mesh axis runs over, the one named last changes fastest.
Arguments:
- features: bfloat16 [12, 4, 256, 256], P(None, 'row', 'col'), may hold values from -6 to 6
Outputs:
- schur: float32 [12, 4, 256, 6, 8, 256], P(None, 'row', None, None, 'col')
- panels: float32 [12, 4, 256, 512], P(None, 'row')
The draws below stay inside these ranges and needn't reach their ends.
All inputs are finite; a program needn't handle non-finite values.
Results may differ from the reference program's by a relative error of at most 0.0033.
Values may be sent and summed in bfloat16 or wider, within the bound.
A program may use at most 128 MiB of HBM per device.

```python
import jax
import jax.numpy as jnp
from jax import lax

TILE = 256
FEAT = 256
TR_DEV = 12
ORDER = 12288
TC_DEV = 6
N_ROW = 4
N_COL = 8


def block_levels(own_key, shape, cuts, least, largest):
    gain = 1.0
    for axis_at, parts in cuts:
        steps = jax.random.uniform(jax.random.fold_in(jax.random.fold_in(own_key, 6), axis_at), (parts,), jnp.float32, least / len(cuts), largest / len(cuts))
        gain = gain * jnp.repeat(jnp.exp(steps), shape[axis_at] // parts).reshape((-1,) + (1,) * (len(shape) - 1 - axis_at))
    return gain


def centred(rng, dims, deviation, reach, cuts=(), kind=jnp.bfloat16):
    level = block_levels(rng, dims, cuts, -0.22, 0.18) if cuts else 1.0
    entries = jax.random.normal(rng, dims, jnp.float32) * deviation * level
    return jnp.minimum(jnp.maximum(entries, -reach), reach).astype(kind)


def setup_inputs(seed: int = 0) -> dict:
    seeds = jax.random.split(jax.random.key(seed), 2)
    features = centred(seeds[0], (TR_DEV, N_ROW, TILE, FEAT), 1.0, 6.0, ((1, 4), (2, 8)))
    return dict(features=features)


kernel_gain = 2.0
epsilon = 1e-06

def kernel_block(row_feats, col_feats, row_start, col_start):
    products = jnp.dot(row_feats.astype(jnp.float32), col_feats.T.astype(jnp.float32), preferred_element_type=jnp.float32)
    values = jnp.exp(kernel_gain * (products - 1.0))
    row_index = row_start + jnp.arange(row_feats.shape[0], dtype=jnp.int32)[:, None]
    col_index = col_start + jnp.arange(col_feats.shape[0], dtype=jnp.int32)[None, :]
    return values + (row_index == col_index).astype(values.dtype)

def panel_factor(column, panel_index):
    start = panel_index * TILE
    factor = jnp.linalg.cholesky(column[start:start + TILE])
    solved = lax.linalg.triangular_solve(factor, column, left_side=False, lower=True, transpose_a=True)
    pieces = solved.reshape(ORDER // TILE, TILE, TILE)
    marker = jnp.arange(ORDER // TILE, dtype=jnp.int32)[:, None, None]
    pieces = jnp.where(marker == panel_index, factor[None], jnp.where(marker < panel_index, jnp.zeros_like(pieces), pieces))
    return pieces.reshape(ORDER, TILE)

def reference(features):
    floated = features.reshape(ORDER, FEAT).astype(jnp.float32)
    unit_rows = (floated * lax.rsqrt(lax.optimization_barrier(jnp.sum(floated * floated, axis=-1, keepdims=True)) + epsilon)).astype(jnp.bfloat16)
    front = kernel_block(unit_rows, unit_rows[:2 * TILE], jnp.int32(0), jnp.int32(0))
    first = panel_factor(front[:, :TILE], 0)
    col_next = front[:, TILE:] - jnp.dot(first, first[TILE:2 * TILE].T, precision=lax.Precision.HIGHEST)
    second = panel_factor(col_next, 1)
    both = jnp.concatenate([first, second], axis=1)

    def one_block(block_index):
        start = (block_index * TILE).astype(jnp.int32)
        row_feats = lax.dynamic_slice_in_dim(unit_rows, start, TILE, 0)
        block_kernel = kernel_block(row_feats, unit_rows, start, jnp.int32(0))
        block_panel = lax.dynamic_slice_in_dim(both, start, TILE, 0)
        return block_kernel - jnp.dot(block_panel, both.T, precision=lax.Precision.HIGHEST)
    schur = lax.map(one_block, jnp.arange(ORDER // TILE, dtype=jnp.int32)).reshape(ORDER, ORDER)
    return (schur.reshape(TR_DEV, N_ROW, TILE, TC_DEV, N_COL, TILE), both.reshape(TR_DEV, N_ROW, TILE, 2 * TILE))
```

```python
import math

import jax
import jax.numpy as jnp
from jax import lax
from jax.experimental import pallas as pl
from jax.experimental.pallas import tpu as pltpu
from jax.sharding import PartitionSpec as P

kernel_gain = 2.0
epsilon = 1e-06
LEAF = 128
SUB = 8
gain2 = kernel_gain / math.log(2.0)
BF = jnp.bfloat16
F32 = jnp.float32
NT = (((1,), (1,)), ((), ()))
NN = (((1,), (0,)), ((), ()))
TN = (((0,), (0,)), ((), ()))


def split(x):
    hi = x.astype(BF)
    return hi, (x - hi.astype(F32)).astype(BF)


def dot(a, b, dims):
    return lax.dot_general(a, b, dims, preferred_element_type=F32)


def dot3(a, b, dims):
    ah, al = a
    bh, bl = b
    return dot(ah, bh, dims) + (dot(ah, bl, dims) + dot(al, bh, dims))


def gram(a, b):
    return jnp.exp2(gain2 * dot(a, b, NT) - gain2)


def eye(n):
    return (
        lax.broadcasted_iota(jnp.int32, (n, n), 0) == lax.broadcasted_iota(jnp.int32, (n, n), 1)
    ).astype(F32)


def leaf(block):
    groups = LEAF // SUB
    ident = eye(LEAF)
    a = [block[g * SUB:(g + 1) * SUB] for g in range(groups)]
    m = [ident[g * SUB:(g + 1) * SUB] for g in range(groups)]
    sub = lax.broadcasted_iota(jnp.int32, (SUB, LEAF), 0)

    def lane(x, at):
        return jnp.broadcast_to(x[:, at:at + 1], (SUB, LEAF))

    def row(x, at):
        return jnp.broadcast_to(x[at:at + 1, :], (SUB, LEAF))

    for p in range(groups):
        ra, rm = a[p], m[p]
        c = [lane(ra, p * SUB + k) for k in range(SUB)]
        scale, ua, um, uc = [], [], [], []
        for j in range(SUB):
            r = lax.rsqrt(row(c[j], j))
            below = jnp.where(sub > j, c[j] * r, 0.0)
            wa, wm = row(ra, j) * r, row(rm, j) * r
            wc = [row(c[k], j) * r for k in range(j + 1, SUB)]
            scale.append(r)
            ua.append(wa)
            um.append(wm)
            uc.append(wc)
            for k in range(j + 1, SUB):
                c[k] = c[k] - below * wc[k - j - 1]
            ra = jnp.where(sub == j, wa, ra - below * wa)
            rm = jnp.where(sub == j, wm, rm - below * wm)
        a[p], m[p] = ra, rm
        for g in range(p + 1, groups):
            c = [lane(a[g], p * SUB + k) for k in range(SUB)]
            for j in range(SUB):
                l = c[j] * scale[j]
                for k in range(j + 1, SUB):
                    c[k] = c[k] - l * uc[j][k - j - 1]
                a[g] = a[g] - l * ua[j]
                m[g] = m[g] - l * um[j]
    return jnp.concatenate(m, axis=0)


def factor_steps(front, work, between):
    n = front.shape[0]
    blocks = n // LEAF
    work[:, 0:n] = gram(front, front) + eye(n)
    work[:, n:2 * n] = eye(n)

    def step(b, carry):
        here = pl.ds(pl.multiple_of(b * LEAF, LEAF), LEAF)
        inverse = leaf(work[here, here])
        for at in range(blocks):
            lo_at, up = at * LEAF, (at + 1) * LEAF

            @pl.when(b == at)
            def _():
                inv = split(inverse)
                if at:
                    work[lo_at:up, n:n + lo_at] = dot3(
                        inv, split(work[lo_at:up, n:n + lo_at]), NN
                    )
                work[lo_at:up, n + lo_at:n + up] = inverse
                if up < n:
                    right = dot3(inv, split(work[lo_at:up, up:n]), NN)
                    rs = split(right)
                    work[up:n, up:n] = work[up:n, up:n] - dot3(rs, rs, TN)
                    ms = split(work[lo_at:up, n:n + up])
                    work[up:n, n:n + up] = work[up:n, n:n + up] - dot3(rs, ms, TN)
                between(at)

        return carry

    lax.fori_loop(0, blocks, step, 0)


def prepare_body(
    features_ref, rows_ref, cols_ref, front_ref, hi_ref, lo_ref, held, slips, work, tall_send,
    tall_recv, slip_send, slip_recv, front_send, front_recv, row_send, row_recv, pass_send,
    pass_recv, col_send, col_recv, keep_sem,
):
    rows = lax.axis_size("row")
    peers = lax.axis_size("col")
    r = lax.axis_index("row")
    c = lax.axis_index("col")
    stride, piece = features_ref.shape[1], features_ref.shape[2]
    tile_len = piece * peers
    pairs = peers // 2
    partner = c + 1 - 2 * lax.rem(c, 2)

    def at_row(d):
        return lax.rem(r + d, rows), c

    def at_col(peer):
        return r, peer

    barrier = pltpu.get_barrier_semaphore()
    for d in range(1, rows):
        pl.semaphore_signal(
            barrier, inc=1, device_id=at_row(d), device_id_type=pl.DeviceIdType.MESH
        )
    for d in range(1, peers):
        pl.semaphore_signal(
            barrier, inc=1, device_id=at_col(lax.rem(c + d, peers)),
            device_id_type=pl.DeviceIdType.MESH,
        )

    floated = features_ref[...].astype(F32)
    total = jnp.sum(floated * floated, axis=-1, keepdims=True)
    held[r] = (floated * lax.rsqrt(total + epsilon)).astype(BF)
    pl.semaphore_wait(barrier, rows + peers - 2)

    def remote(src, dst, send, recv, target):
        return pltpu.make_async_remote_copy(
            src_ref=src, dst_ref=dst, send_sem=send, recv_sem=recv, device_id=target,
            device_id_type=pl.DeviceIdType.MESH,
        )

    def strip(peer):
        return pl.ds(pl.multiple_of(peer * piece, piece), piece)

    here = strip(c)

    def slip(tile, d, target):
        return remote(
            held.at[tile, 0, 0], slips.at[tile], slip_send.at[tile, d], slip_recv.at[tile], target
        )

    for tile in range(2):
        @pl.when(r == tile)
        def _():
            for d in range(1, rows):
                slip(tile, d, at_row(d)).start()
            own = pltpu.make_async_copy(held.at[tile, 0, 0], slips.at[tile], keep_sem.at[0])
            own.start()
            own.wait()

    def tall(slot, d, target):
        return remote(held.at[slot], held.at[slot], tall_send.at[d], tall_recv.at[d], target)

    for d in range(1, rows):
        tall(r, d, at_row(d)).start()

    for tile in range(2):
        @pl.when(r != tile)
        def _():
            slip(tile, 1, at_row(1)).wait_recv()

    def front_copy(d, owner, target):
        return remote(
            slips, front_ref.at[:, strip(owner)], front_send.at[d], front_recv.at[d], target
        )

    for d in range(1, peers):
        front_copy(d, c, at_col(lax.rem(c + d, peers))).start()
    kept = [
        pltpu.make_async_copy(slips, front_ref.at[:, here], keep_sem.at[0]),
        pltpu.make_async_copy(held.at[r], rows_ref.at[:, :, here], keep_sem.at[1]),
    ]
    for copy in kept:
        copy.start()

    def row_copy(d, owner, target):
        return remote(
            held.at[r], rows_ref.at[:, :, strip(owner)], row_send.at[d], row_recv.at[d], target
        )

    def pass_copy(d, owner, target):
        there = rows_ref.at[:, :, strip(owner)]
        return remote(there, there, pass_send.at[d], pass_recv.at[d], target)

    row_copy(0, c, at_col(partner)).start()
    for d in range(1, pairs):
        row_copy(d, c, at_col(lax.rem(c + 2 * d, peers))).start()

    def col_copy(block, turn, owner, target):
        away = lax.rem(target - owner + peers, peers)
        return remote(
            held.at[block, :, turn], cols_ref.at[:, strip(owner)], col_send.at[away],
            col_recv.at[away], at_col(target),
        )

    def hand_out(block):
        for turn in range(stride):
            peer = block + turn * rows

            @pl.when(peer != c)
            def _():
                col_copy(block, turn, c, peer).start()

            @pl.when(peer == c)
            def _():
                pltpu.make_async_copy(
                    held.at[block, :, turn], cols_ref.at[:, here], keep_sem.at[2]
                ).start()

    hand_out(r)
    for d in range(1, peers):
        front_copy(d, lax.rem(c - d + peers, peers), at_col(c)).wait_recv()
    kept[0].wait()

    def between(at):
        d = at + 1
        if d < rows:
            block = lax.rem(r - d + rows, rows)
            tall(block, d, at_row(d)).wait_recv()
            hand_out(block)
        if at == min(2, rows - 2):
            for d in range(1, pairs):
                owner = lax.rem(c - 2 * d + peers, peers)
                row_copy(d, owner, at_col(partner)).wait_recv()
                pass_copy(d, owner, at_col(partner)).start()

    front = front_ref[...].reshape(2 * tile_len, front_ref.shape[2])
    factor_steps(front, work, between)
    n = front.shape[0]
    for d in range(n // LEAF + 1, rows):
        block = lax.rem(r - d + rows, rows)
        tall(block, d, at_row(d)).wait_recv()
        hand_out(block)
    hi, lo = split(work[:, n:2 * n])
    hi_ref[...] = hi
    lo_ref[...] = lo

    kept[1].wait()
    pltpu.make_async_copy(
        held.at[lax.rem(c, rows), :, c // rows], cols_ref.at[:, here], keep_sem.at[2]
    ).wait()
    row_copy(0, partner, at_col(partner)).wait_recv()
    row_copy(0, c, at_col(partner)).wait_send()
    for d in range(1, pairs):
        owner = lax.rem(partner - 2 * d + peers, peers)
        pass_copy(d, owner, at_col(partner)).wait_recv()
        pass_copy(d, lax.rem(c - 2 * d + peers, peers), at_col(partner)).wait_send()
        row_copy(d, c, at_col(partner)).wait_send()
    for d in range(1, peers):
        col_copy(0, 0, lax.rem(c - d + peers, peers), c).wait_recv()
        col_copy(0, 0, c, lax.rem(c + d, peers)).wait_send()
        front_copy(d, c, at_col(partner)).wait_send()
    for d in range(1, rows):
        tall(r, d, at_row(d)).wait_send()
    for tile in range(2):
        @pl.when(r == tile)
        def _():
            for d in range(1, rows):
                slip(tile, d, at_row(d)).wait_send()


def prepare(features, row_count, col_count):
    local_tiles, piece, feat = features.shape
    stride = col_count // row_count
    across = local_tiles // stride
    tile_len = piece * col_count
    n = 2 * tile_len
    dma = pltpu.SemaphoreType.DMA
    anywhere = pl.BlockSpec(memory_space=pl.ANY)
    vmem = pl.BlockSpec(memory_space=pltpu.VMEM)
    return pl.pallas_call(
        prepare_body,
        out_shape=(
            jax.ShapeDtypeStruct((across, stride, tile_len, feat), BF),
            jax.ShapeDtypeStruct((across, tile_len, feat), BF),
            jax.ShapeDtypeStruct((2, tile_len, feat), BF),
            jax.ShapeDtypeStruct((n, n), BF),
            jax.ShapeDtypeStruct((n, n), BF),
        ),
        in_specs=[vmem],
        out_specs=(anywhere, anywhere, vmem, vmem, vmem),
        scratch_shapes=[
            pltpu.VMEM((row_count, across, stride, piece, feat), BF),
            pltpu.VMEM((2, piece, feat), BF),
            pltpu.VMEM((n, 2 * n), F32),
            dma((row_count,)), dma((row_count,)), dma((2, row_count)), dma((2,)),
            dma((col_count,)), dma((col_count,)), dma((col_count,)), dma((col_count,)),
            dma((col_count,)), dma((col_count,)), dma((col_count,)), dma((col_count,)), dma((3,)),
        ],
        compiler_params=pltpu.CompilerParams(
            collective_id=0, has_side_effects=True, vmem_limit_bytes=48 * 2**20
        ),
        cost_estimate=pl.CostEstimate(flops=int(2e10), bytes_accessed=int(5e7), transcendentals=0),
        name="prepare",
    )(features.reshape(across, stride, piece, feat))


def panel_of(points, tile_id, front, hi_ref, lo_ref, tile_len):
    n = front.shape[0]
    values = gram(points, front)
    at = lax.broadcasted_iota(jnp.int32, values.shape, 0) + tile_id * tile_len
    values = values + (at == lax.broadcasted_iota(jnp.int32, values.shape, 1)).astype(F32)
    hi, lo = split(values)
    t = tile_len
    first = dot3((hi[:, :t], lo[:, :t]), (hi_ref[:t, :t], lo_ref[:t, :t]), NT)
    second = dot3((hi, lo), (hi_ref[t:, :], lo_ref[t:, :]), NT)
    return jnp.concatenate([first, second], axis=1)


def schur_body(rows_ref, cols_ref, front_ref, hi_ref, lo_ref, out_ref, panel_ref, q_ref):
    tile_len = rows_ref.shape[0]
    across = cols_ref.shape[0] // tile_len
    own_row, own_col = lax.axis_index("row"), lax.axis_index("col")
    row_count, col_count = lax.axis_size("row"), lax.axis_size("col")
    a = pl.program_id(0)
    chunks = across * tile_len // LEAF

    @pl.when(a == 0)
    def _():
        def one(b, carry):
            here = pl.ds(pl.multiple_of(b * tile_len, tile_len), tile_len)
            hi, lo = split(
                panel_of(
                    cols_ref[here, :], b * col_count + own_col, front_ref[...], hi_ref, lo_ref,
                    tile_len,
                )
            )
            q_ref[here, :] = jnp.concatenate([hi, lo[:, :LEAF], hi[:, :LEAF]], axis=1)
            return carry

        lax.fori_loop(0, across, one, 0, unroll=True)

    tile_id = a * row_count + own_row
    points = rows_ref[...]
    panel = panel_of(points, tile_id, front_ref[...], hi_ref, lo_ref, tile_len)
    panel_ref[...] = panel
    hi, lo = split(panel)
    p = jnp.concatenate([hi, hi[:, :LEAF], lo[:, :LEAF]], axis=1)
    per = tile_len // LEAF
    s = gram(points, cols_ref[...]) - dot(p, q_ref[...], NT)
    for k in range(chunks):
        out_ref[pl.ds(k, tile_len, stride=chunks), :] = s[:, k * LEAF:(k + 1) * LEAF]

    for b in range(across):
        @pl.when(tile_id == b * col_count + own_col)
        def _():
            ident = eye(tile_len)
            for k in range(per):
                at = pl.ds(b * per + k, tile_len, stride=chunks)
                out_ref[at, :] = out_ref[at, :] + ident[:, k * LEAF:(k + 1) * LEAF]


def schur(row_points, col_points, front, hi, lo, tile_len):
    rows, feat = row_points.shape
    cols = col_points.shape[0]
    n = front.shape[0]
    chunks = cols // LEAF

    def whole(shape):
        return pl.BlockSpec(shape, lambda a: (0, 0))

    return pl.pallas_call(
        schur_body,
        out_shape=(
            jax.ShapeDtypeStruct((rows * chunks, LEAF), F32),
            jax.ShapeDtypeStruct((rows, n), F32),
        ),
        grid=(rows // tile_len,),
        in_specs=[
            pl.BlockSpec((tile_len, feat), lambda a: (a, 0)),
            whole((cols, feat)),
            whole((n, feat)),
            whole((n, n)),
            whole((n, n)),
        ],
        out_specs=(
            pl.BlockSpec((tile_len * chunks, LEAF), lambda a: (a, 0)),
            pl.BlockSpec((tile_len, n), lambda a: (a, 0)),
        ),
        scratch_shapes=[pltpu.VMEM((cols, n + 2 * LEAF), BF)],
        compiler_params=pltpu.CompilerParams(
            dimension_semantics=("arbitrary",), vmem_limit_bytes=48 * 2**20
        ),
        name="schur",
    )(row_points, col_points, front, hi, lo)


def per_device(features):
    row_count = lax.axis_size("row")
    col_count = lax.axis_size("col")
    local_tiles, _, piece, feat = features.shape
    tile_len = piece * col_count
    rows, cols, leading, hi, lo = prepare(features[:, 0], row_count, col_count)
    front = leading.reshape(2 * tile_len, feat)
    row_points = rows.reshape(-1, feat)
    col_points = cols.reshape(-1, feat)
    big, panels = schur(row_points, col_points, front, hi, lo, tile_len)
    across = col_points.shape[0] // tile_len
    return (
        big.reshape(local_tiles, 1, tile_len, across, 1, tile_len),
        panels.reshape(local_tiles, 1, tile_len, 2 * tile_len),
    )


def solution(mesh):
    return jax.shard_map(
        per_device,
        mesh=mesh,
        in_specs=(P(None, "row", "col", None),),
        out_specs=(P(None, "row", None, None, "col", None), P(None, "row", None, None)),
        check_vma=False,
    )
```

```python
import math

import jax
import jax.numpy as jnp
from jax import lax
from jax.experimental import pallas as pl
from jax.experimental.pallas import tpu as pltpu
from jax.sharding import PartitionSpec as P

kernel_gain = 2.0
epsilon = 1e-06
LEAF = 128
SUB = 8
gain2 = kernel_gain / math.log(2.0)
BF = jnp.bfloat16
F32 = jnp.float32
NT = (((1,), (1,)), ((), ()))
NN = (((1,), (0,)), ((), ()))
TN = (((0,), (0,)), ((), ()))


def split(x):
    hi = x.astype(BF)
    return hi, (x - hi.astype(F32)).astype(BF)


def dot(a, b, dims):
    return lax.dot_general(a, b, dims, preferred_element_type=F32)


def dot3(a, b, dims):
    ah, al = a
    bh, bl = b
    return dot(ah, bh, dims) + (dot(ah, bl, dims) + dot(al, bh, dims))


def gram(a, b):
    return jnp.exp2(gain2 * dot(a, b, NT) - gain2)


def eye(n):
    return (
        lax.broadcasted_iota(jnp.int32, (n, n), 0) == lax.broadcasted_iota(jnp.int32, (n, n), 1)
    ).astype(F32)


def leaf(block):
    groups = LEAF // SUB
    ident = eye(LEAF)
    a = [block[g * SUB:(g + 1) * SUB] for g in range(groups)]
    m = [ident[g * SUB:(g + 1) * SUB] for g in range(groups)]
    sub = lax.broadcasted_iota(jnp.int32, (SUB, LEAF), 0)

    def lane(x, at):
        return jnp.broadcast_to(x[:, at:at + 1], (SUB, LEAF))

    def row(x, at):
        return jnp.broadcast_to(x[at:at + 1, :], (SUB, LEAF))

    for p in range(groups):
        ra, rm = a[p], m[p]
        c = [lane(ra, p * SUB + k) for k in range(SUB)]
        scale, ua, um, uc = [], [], [], []
        for j in range(SUB):
            r = lax.rsqrt(row(c[j], j))
            below = jnp.where(sub > j, c[j] * r, 0.0)
            wa, wm = row(ra, j) * r, row(rm, j) * r
            wc = [row(c[k], j) * r for k in range(j + 1, SUB)]
            scale.append(r)
            ua.append(wa)
            um.append(wm)
            uc.append(wc)
            for k in range(j + 1, SUB):
                c[k] = c[k] - below * wc[k - j - 1]
            ra = jnp.where(sub == j, wa, ra - below * wa)
            rm = jnp.where(sub == j, wm, rm - below * wm)
        a[p], m[p] = ra, rm
        for g in range(p + 1, groups):
            c = [lane(a[g], p * SUB + k) for k in range(SUB)]
            for j in range(SUB):
                l = c[j] * scale[j]
                for k in range(j + 1, SUB):
                    c[k] = c[k] - l * uc[j][k - j - 1]
                a[g] = a[g] - l * ua[j]
                m[g] = m[g] - l * um[j]
    return jnp.concatenate(m, axis=0)


def factor_steps(front, work, between):
    n = front.shape[0]
    blocks = n // LEAF
    work[:, 0:n] = gram(front, front) + eye(n)
    work[:, n:2 * n] = eye(n)

    def step(b, carry):
        here = pl.ds(pl.multiple_of(b * LEAF, LEAF), LEAF)
        inverse = leaf(work[here, here])
        for at in range(blocks):
            lo_at, up = at * LEAF, (at + 1) * LEAF

            @pl.when(b == at)
            def _():
                inv = split(inverse)
                if at:
                    work[lo_at:up, n:n + lo_at] = dot3(
                        inv, split(work[lo_at:up, n:n + lo_at]), NN
                    )
                work[lo_at:up, n + lo_at:n + up] = inverse
                if up < n:
                    right = dot3(inv, split(work[lo_at:up, up:n]), NN)
                    rs = split(right)
                    work[up:n, up:n] = work[up:n, up:n] - dot3(rs, rs, TN)
                    ms = split(work[lo_at:up, n:n + up])
                    work[up:n, n:n + up] = work[up:n, n:n + up] - dot3(rs, ms, TN)
                between(at)

        return carry

    lax.fori_loop(0, blocks, step, 0)


def prepare_body(
    features_ref, rows_ref, cols_ref, front_ref, hi_ref, lo_ref, held, slips, work, tall_send,
    tall_recv, slip_send, slip_recv, front_send, front_recv, row_send, row_recv, pass_send,
    pass_recv, col_send, col_recv, keep_sem,
):
    rows = lax.axis_size("row")
    peers = lax.axis_size("col")
    r = lax.axis_index("row")
    c = lax.axis_index("col")
    stride, piece = features_ref.shape[1], features_ref.shape[2]
    tile_len = piece * peers
    pairs = peers // 2
    partner = c + 1 - 2 * lax.rem(c, 2)

    def at_row(d):
        return lax.rem(r + d, rows), c

    def at_col(peer):
        return r, peer

    barrier = pltpu.get_barrier_semaphore()
    for d in range(1, rows):
        pl.semaphore_signal(
            barrier, inc=1, device_id=at_row(d), device_id_type=pl.DeviceIdType.MESH
        )
    for d in range(1, peers):
        pl.semaphore_signal(
            barrier, inc=1, device_id=at_col(lax.rem(c + d, peers)),
            device_id_type=pl.DeviceIdType.MESH,
        )

    floated = features_ref[...].astype(F32)
    total = jnp.sum(floated * floated, axis=-1, keepdims=True)
    held[r] = (floated * lax.rsqrt(total + epsilon)).astype(BF)
    pl.semaphore_wait(barrier, rows + peers - 2)

    def remote(src, dst, send, recv, target):
        return pltpu.make_async_remote_copy(
            src_ref=src, dst_ref=dst, send_sem=send, recv_sem=recv, device_id=target,
            device_id_type=pl.DeviceIdType.MESH,
        )

    def strip(peer):
        return pl.ds(pl.multiple_of(peer * piece, piece), piece)

    here = strip(c)

    def slip(tile, d, target):
        return remote(
            held.at[tile, 0, 0], slips.at[tile], slip_send.at[tile, d], slip_recv.at[tile], target
        )

    for tile in range(2):
        @pl.when(r == tile)
        def _():
            for d in range(1, rows):
                slip(tile, d, at_row(d)).start()
            own = pltpu.make_async_copy(held.at[tile, 0, 0], slips.at[tile], keep_sem.at[0])
            own.start()
            own.wait()

    def up(step, owner, target):
        return remote(
            held.at[owner], held.at[owner], tall_send.at[0, step], tall_recv.at[0, step],
            (target, c),
        )

    def down(step, owner, target):
        return remote(
            held.at[owner], held.at[owner], tall_send.at[1, step], tall_recv.at[1, step],
            (target, c),
        )

    def hop(step):
        @pl.when((r + 1 < rows) & (r - step >= 0))
        def _():
            up(step, r - step, r + 1).start()

        @pl.when((r - 1 >= 0) & (r + step < rows))
        def _():
            down(step, r + step, r - 1).start()

    hop(0)

    for tile in range(2):
        @pl.when(r != tile)
        def _():
            slip(tile, 1, at_row(1)).wait_recv()

    def front_copy(d, owner, target):
        return remote(
            slips, front_ref.at[:, strip(owner)], front_send.at[d], front_recv.at[d], target
        )

    for d in range(1, peers):
        front_copy(d, c, at_col(lax.rem(c + d, peers))).start()
    kept = [
        pltpu.make_async_copy(slips, front_ref.at[:, here], keep_sem.at[0]),
        pltpu.make_async_copy(held.at[r], rows_ref.at[:, :, here], keep_sem.at[1]),
    ]
    for copy in kept:
        copy.start()

    def row_copy(d, owner, target):
        return remote(
            held.at[r], rows_ref.at[:, :, strip(owner)], row_send.at[d], row_recv.at[d], target
        )

    def pass_copy(d, owner, target):
        there = rows_ref.at[:, :, strip(owner)]
        return remote(there, there, pass_send.at[d], pass_recv.at[d], target)


    def col_copy(block, turn, owner, target):
        away = lax.rem(target - owner + peers, peers)
        return remote(
            held.at[block, :, turn], cols_ref.at[:, strip(owner)], col_send.at[away],
            col_recv.at[away], at_col(target),
        )

    def hand_out(block):
        for turn in range(stride):
            peer = block + turn * rows

            @pl.when(peer != c)
            def _():
                col_copy(block, turn, c, peer).start()

            @pl.when(peer == c)
            def _():
                pltpu.make_async_copy(
                    held.at[block, :, turn], cols_ref.at[:, here], keep_sem.at[2]
                ).start()

    def arrive(step):
        @pl.when(r - 1 - step >= 0)
        def _():
            up(step, r - 1 - step, r - 1).wait_recv()

        @pl.when(r + 1 + step < rows)
        def _():
            down(step, r + 1 + step, r + 1).wait_recv()

        if step + 2 < rows:
            hop(step + 1)

    def share(step):
        @pl.when(r - 1 - step >= 0)
        def _():
            hand_out(r - 1 - step)

        @pl.when(r + 1 + step < rows)
        def _():
            hand_out(r + 1 + step)

    arrive(0)
    share(0)
    for d in range(1, peers):
        front_copy(d, lax.rem(c - d + peers, peers), at_col(c)).wait_recv()
    kept[0].wait()
    row_copy(0, c, at_col(partner)).start()
    for d in range(1, pairs):
        row_copy(d, c, at_col(lax.rem(c + 2 * d, peers))).start()

    def pass_on():
        for d in range(1, pairs):
            owner = lax.rem(c - 2 * d + peers, peers)
            row_copy(d, owner, at_col(partner)).wait_recv()
            pass_copy(d, owner, at_col(partner)).start()

    def between(at):
        if at < rows - 2:
            arrive(at + 1)
            share(at + 1)
        if at == 2:
            pass_on()

    front = front_ref[...].reshape(2 * tile_len, front_ref.shape[2])
    factor_steps(front, work, between)
    n = front.shape[0]
    for step in range(n // LEAF + 1, rows - 1):
        arrive(step)
        share(step)
    hi, lo = split(work[:, n:2 * n])
    hi_ref[...] = hi
    lo_ref[...] = lo

    kept[1].wait()
    row_copy(0, partner, at_col(partner)).wait_recv()
    row_copy(0, c, at_col(partner)).wait_send()
    for d in range(1, pairs):
        owner = lax.rem(partner - 2 * d + peers, peers)
        pass_copy(d, owner, at_col(partner)).wait_recv()
        pass_copy(d, lax.rem(c - 2 * d + peers, peers), at_col(partner)).wait_send()
        row_copy(d, c, at_col(partner)).wait_send()
    for d in range(1, peers):
        front_copy(d, c, at_col(partner)).wait_send()

    own_cols = pltpu.make_async_copy(rows_ref.at[:, c // rows], cols_ref, keep_sem.at[2])

    @pl.when(lax.rem(c, rows) == r)
    def _():
        own_cols.start()
        own_cols.wait()

    @pl.when(lax.rem(c, rows) != r)
    def _():
        pltpu.make_async_copy(held.at[0, :, 0], cols_ref.at[:, here], keep_sem.at[2]).wait()
        for d in range(1, peers):
            col_copy(0, 0, lax.rem(c - d + peers, peers), c).wait_recv()
    for d in range(1, peers):
        @pl.when(lax.rem(lax.rem(c + d, peers), rows) != r)
        def _():
            col_copy(0, 0, c, lax.rem(c + d, peers)).wait_send()
    for step in range(rows - 1):
        @pl.when((r + 1 < rows) & (r - step >= 0))
        def _():
            up(step, r, r + 1).wait_send()

        @pl.when((r - 1 >= 0) & (r + step < rows))
        def _():
            down(step, r, r - 1).wait_send()
    for tile in range(2):
        @pl.when(r == tile)
        def _():
            for d in range(1, rows):
                slip(tile, d, at_row(d)).wait_send()


def prepare(features, row_count, col_count):
    local_tiles, piece, feat = features.shape
    stride = col_count // row_count
    across = local_tiles // stride
    tile_len = piece * col_count
    n = 2 * tile_len
    dma = pltpu.SemaphoreType.DMA
    anywhere = pl.BlockSpec(memory_space=pl.ANY)
    vmem = pl.BlockSpec(memory_space=pltpu.VMEM)
    return pl.pallas_call(
        prepare_body,
        out_shape=(
            jax.ShapeDtypeStruct((across, stride, tile_len, feat), BF),
            jax.ShapeDtypeStruct((across, tile_len, feat), BF),
            jax.ShapeDtypeStruct((2, tile_len, feat), BF),
            jax.ShapeDtypeStruct((n, n), BF),
            jax.ShapeDtypeStruct((n, n), BF),
        ),
        in_specs=[vmem],
        out_specs=(anywhere, anywhere, vmem, vmem, vmem),
        scratch_shapes=[
            pltpu.VMEM((row_count, across, stride, piece, feat), BF),
            pltpu.VMEM((2, piece, feat), BF),
            pltpu.VMEM((n, 2 * n), F32),
            dma((2, row_count)), dma((2, row_count)), dma((2, row_count)), dma((2,)),
            dma((col_count,)), dma((col_count,)), dma((col_count,)), dma((col_count,)),
            dma((col_count,)), dma((col_count,)), dma((col_count,)), dma((col_count,)), dma((3,)),
        ],
        compiler_params=pltpu.CompilerParams(
            collective_id=0, has_side_effects=True, vmem_limit_bytes=48 * 2**20
        ),
        cost_estimate=pl.CostEstimate(flops=int(2e10), bytes_accessed=int(5e7), transcendentals=0),
        name="prepare",
    )(features.reshape(across, stride, piece, feat))


def panel_of(points, tile_id, front, hi_ref, lo_ref, tile_len):
    n = front.shape[0]
    values = gram(points, front)
    at = lax.broadcasted_iota(jnp.int32, values.shape, 0) + tile_id * tile_len
    values = values + (at == lax.broadcasted_iota(jnp.int32, values.shape, 1)).astype(F32)
    hi, lo = split(values)
    t = tile_len
    first = dot3((hi[:, :t], lo[:, :t]), (hi_ref[:t, :t], lo_ref[:t, :t]), NT)
    second = dot3((hi, lo), (hi_ref[t:, :], lo_ref[t:, :]), NT)
    return jnp.concatenate([first, second], axis=1)


def schur_body(rows_ref, cols_ref, front_ref, hi_ref, lo_ref, out_ref, panel_ref, q_ref):
    tile_len = rows_ref.shape[0]
    across = cols_ref.shape[0] // tile_len
    own_row, own_col = lax.axis_index("row"), lax.axis_index("col")
    row_count, col_count = lax.axis_size("row"), lax.axis_size("col")
    a = pl.program_id(0)
    chunks = across * tile_len // LEAF

    @pl.when(a == 0)
    def _():
        def one(b, carry):
            here = pl.ds(pl.multiple_of(b * tile_len, tile_len), tile_len)
            hi, lo = split(
                panel_of(
                    cols_ref[here, :], b * col_count + own_col, front_ref[...], hi_ref, lo_ref,
                    tile_len,
                )
            )
            q_ref[here, :] = jnp.concatenate([hi, lo[:, :LEAF], hi[:, :LEAF]], axis=1)
            return carry

        lax.fori_loop(0, across, one, 0, unroll=True)

    tile_id = a * row_count + own_row
    points = rows_ref[...]
    panel = panel_of(points, tile_id, front_ref[...], hi_ref, lo_ref, tile_len)
    panel_ref[...] = panel
    hi, lo = split(panel)
    p = jnp.concatenate([hi, hi[:, :LEAF], lo[:, :LEAF]], axis=1)
    per = tile_len // LEAF
    s = gram(points, cols_ref[...]) - dot(p, q_ref[...], NT)
    for k in range(chunks):
        out_ref[pl.ds(k, tile_len, stride=chunks), :] = s[:, k * LEAF:(k + 1) * LEAF]

    for b in range(across):
        @pl.when(tile_id == b * col_count + own_col)
        def _():
            ident = eye(tile_len)
            for k in range(per):
                at = pl.ds(b * per + k, tile_len, stride=chunks)
                out_ref[at, :] = out_ref[at, :] + ident[:, k * LEAF:(k + 1) * LEAF]


def schur(row_points, col_points, front, hi, lo, tile_len):
    rows, feat = row_points.shape
    cols = col_points.shape[0]
    n = front.shape[0]
    chunks = cols // LEAF

    def whole(shape):
        return pl.BlockSpec(shape, lambda a: (0, 0))

    return pl.pallas_call(
        schur_body,
        out_shape=(
            jax.ShapeDtypeStruct((rows * chunks, LEAF), F32),
            jax.ShapeDtypeStruct((rows, n), F32),
        ),
        grid=(rows // tile_len,),
        in_specs=[
            pl.BlockSpec((tile_len, feat), lambda a: (a, 0)),
            whole((cols, feat)),
            whole((n, feat)),
            whole((n, n)),
            whole((n, n)),
        ],
        out_specs=(
            pl.BlockSpec((tile_len * chunks, LEAF), lambda a: (a, 0)),
            pl.BlockSpec((tile_len, n), lambda a: (a, 0)),
        ),
        scratch_shapes=[pltpu.VMEM((cols, n + 2 * LEAF), BF)],
        compiler_params=pltpu.CompilerParams(
            dimension_semantics=("arbitrary",), vmem_limit_bytes=48 * 2**20
        ),
        name="schur",
    )(row_points, col_points, front, hi, lo)


def per_device(features):
    row_count = lax.axis_size("row")
    col_count = lax.axis_size("col")
    local_tiles, _, piece, feat = features.shape
    tile_len = piece * col_count
    rows, cols, leading, hi, lo = prepare(features[:, 0], row_count, col_count)
    front = leading.reshape(2 * tile_len, feat)
    row_points = rows.reshape(-1, feat)
    col_points = cols.reshape(-1, feat)
    big, panels = schur(row_points, col_points, front, hi, lo, tile_len)
    across = col_points.shape[0] // tile_len
    return (
        big.reshape(local_tiles, 1, tile_len, across, 1, tile_len),
        panels.reshape(local_tiles, 1, tile_len, 2 * tile_len),
    )


def solution(mesh):
    return jax.shard_map(
        per_device,
        mesh=mesh,
        in_specs=(P(None, "row", "col", None),),
        out_specs=(P(None, "row", None, None, "col", None), P(None, "row", None, None)),
        check_vma=False,
    )
```

```python
import math

import jax
import jax.numpy as jnp
from jax import lax
from jax.experimental import pallas as pl
from jax.experimental.pallas import tpu as pltpu
from jax.sharding import PartitionSpec as P

kernel_gain = 2.0
epsilon = 1e-06
LEAF = 128
SUB = 16
gain2 = kernel_gain / math.log(2.0)
BF = jnp.bfloat16
F32 = jnp.float32
NT = (((1,), (1,)), ((), ()))
NN = (((1,), (0,)), ((), ()))
TN = (((0,), (0,)), ((), ()))


def split(x):
    hi = x.astype(BF)
    return hi, (x - hi.astype(F32)).astype(BF)


def dot(a, b, dims):
    return lax.dot_general(a, b, dims, preferred_element_type=F32)


def dot3(a, b, dims):
    ah, al = a
    bh, bl = b
    return dot(ah, bh, dims) + (dot(ah, bl, dims) + dot(al, bh, dims))


def gram(a, b):
    return jnp.exp2(gain2 * dot(a, b, NT) - gain2)


def eye(n):
    return (
        lax.broadcasted_iota(jnp.int32, (n, n), 0) == lax.broadcasted_iota(jnp.int32, (n, n), 1)
    ).astype(F32)


def half_leaf(block, sides):
    size = block.shape[0]
    groups = size // SUB
    x = [[m[g * SUB:(g + 1) * SUB] for g in range(groups)] for m in (block, *sides)]
    sub = lax.broadcasted_iota(jnp.int32, (SUB, LEAF), 0)

    def lane(v, at):
        return jnp.broadcast_to(v[:, at:at + 1], (SUB, LEAF))

    def row(v, at):
        return jnp.broadcast_to(v[at:at + 1, :], v.shape)

    for p in range(groups):
        c = [lane(x[0][p], p * SUB + k) for k in range(SUB)]
        pairs = []
        for j in range(0, SUB, 2):
            a, e, f = row(c[j], j), row(c[j], j + 1), row(c[j + 1], j + 1)
            r1, rd = lax.rsqrt(a), lax.rsqrt(a * f - e * e)
            across = e * r1
            r2 = a * r1 * rd
            l1 = c[j] * r1
            l2 = (c[j + 1] - l1 * across) * r2
            u1 = {k: row(l1, k) for k in range(j + 2, SUB)}
            u2 = {k: row(l2, k) for k in range(j + 2, SUB)}
            for k in range(j + 2, SUB):
                c[k] = c[k] - l1 * u1[k] - l2 * u2[k]
            b1 = jnp.where(sub > j + 1, l1, 0.0)
            b2 = jnp.where(sub > j + 1, l2, 0.0)
            w = []
            for m in x:
                w1 = row(m[p], j) * r1
                w2 = (row(m[p], j + 1) - w1 * across) * r2
                m[p] = jnp.where(
                    sub == j, w1, jnp.where(sub == j + 1, w2, m[p] - b1 * w1 - b2 * w2)
                )
                w.append((w1, w2))
            pairs.append((j, r1, across, r2, u1, u2, w))
        for g in range(p + 1, groups):
            c = [lane(x[0][g], p * SUB + k) for k in range(SUB)]
            for j, r1, across, r2, u1, u2, w in pairs:
                l1 = c[j] * r1
                l2 = (c[j + 1] - l1 * across) * r2
                for k in range(j + 2, SUB):
                    c[k] = c[k] - l1 * u1[k] - l2 * u2[k]
                for m, (w1, w2) in zip(x, w):
                    m[g] = m[g] - l1 * w1 - l2 * w2
    return [jnp.concatenate(m, axis=0) for m in x]


def leaf(block):
    h = LEAF // 2
    ident = eye(LEAF)
    upper, first = half_leaf(block[:h], [ident[:h]])
    right = jnp.where(lax.broadcasted_iota(jnp.int32, (h, LEAF), 1) >= h, upper, 0.0)
    rs = split(right)
    lower = block[h:] - dot3(rs, rs, TN)[h:]
    cross = dot3(rs, split(first), TN)[h:]
    packed = pltpu.roll(lower, h, 1)
    wide = lax.broadcasted_iota(jnp.int32, (h, LEAF), 1)
    packed = jnp.where(wide < h, packed, ident[:h][:, :])
    packed = jnp.where(wide < h, packed, pltpu.roll(ident[:h], h, 1))
    done = half_leaf(packed, [])[0]
    second = jnp.where(wide >= h, done, 0.0)
    inner = pltpu.roll(second, h, 1)
    low = second - dot3(split(inner), split(jnp.concatenate([cross, jnp.zeros_like(cross)], axis=0)), NN)
    return jnp.concatenate([first, low], axis=0)


def factor_steps(front, work, between):
    n = front.shape[0]
    blocks = n // LEAF
    spans = [slice(b * LEAF, (b + 1) * LEAF) for b in range(blocks)]
    m_spans = [slice(n + b * LEAF, n + (b + 1) * LEAF) for b in range(blocks)]
    for b in range(blocks):
        work[spans[b], b * LEAF:n] = gram(front[spans[b]], front[b * LEAF:])
    ident = eye(LEAF)
    block = work[spans[0], spans[0]] + ident
    for b in range(blocks):
        inverse = leaf(block)
        inv = split(inverse)
        work[spans[b], m_spans[b]] = inverse
        up = (b + 1) * LEAF
        if up < n:
            rs = split(dot3(inv, split(work[spans[b], up:n]), NN))
            rest = [tuple(v[:, i * LEAF:(i + 1) * LEAF] for v in rs) for i in range(blocks - b - 1)]
            block = work[spans[b + 1], spans[b + 1]] + ident - dot3(rest[0], rest[0], TN)
        between(b)
        if b:
            left = dot3(inv, split(work[spans[b], n:n + b * LEAF]), NN)
            work[spans[b], n:n + b * LEAF] = left
        if up < n:
            ms = split(work[spans[b], n:n + up])
            for i in range(b + 1, blocks):
                ri = rest[i - b - 1]
                at = i * LEAF
                if i > b + 1:
                    ahead = tuple(v[:, (i - b - 1) * LEAF:] for v in rs)
                    work[spans[i], at:n] = work[spans[i], at:n] - dot3(ri, ahead, TN)
                elif i + 1 < blocks:
                    ahead = tuple(v[:, LEAF:] for v in rs)
                    work[spans[i], at + LEAF:n] = work[spans[i], at + LEAF:n] - dot3(ri, ahead, TN)
                change = dot3(ri, ms, TN)
                if b:
                    old = slice(n, n + b * LEAF)
                    work[spans[i], old] = work[spans[i], old] - change[:, :b * LEAF]
                work[spans[i], m_spans[b]] = -change[:, b * LEAF:]
    for b in range(blocks):
        if b + 1 < blocks:
            work[spans[b], n + (b + 1) * LEAF:2 * n] = jnp.zeros((LEAF, n - (b + 1) * LEAF), F32)


def panel_steps(points, tile_id, front, hi_ref, lo_ref, keep):
    t = points.shape[0]
    values = gram(points, front)
    at = lax.broadcasted_iota(jnp.int32, values.shape, 0) + tile_id * t
    values = values + (at == lax.broadcasted_iota(jnp.int32, values.shape, 1)).astype(F32)
    hi, lo = split(values)
    yield
    first = dot3((hi[:, :t], lo[:, :t]), (hi_ref[:t, :t], lo_ref[:t, :t]), NT)
    yield
    second = dot3((hi, lo), (hi_ref[t:, :], lo_ref[t:, :]), NT)
    yield
    keep(first, second)
    yield


def together(steps):
    for _ in zip(*steps):
        pass


def prepare_body(
    features_ref, rows_ref, cols_ref, panel_ref, p_ref, q_ref, held, slips, front_ref, hi_ref,
    lo_ref, work, tall_send,
    tall_recv, slip_send, slip_recv, front_send, front_recv, row_send, row_recv, pass_send,
    pass_recv, col_send, col_recv, keep_sem,
):
    rows = lax.axis_size("row")
    peers = lax.axis_size("col")
    r = lax.axis_index("row")
    c = lax.axis_index("col")
    stride, piece = features_ref.shape[1], features_ref.shape[2]
    tile_len = piece * peers
    pairs = peers // 2
    partner = c + 1 - 2 * lax.rem(c, 2)

    def at_row(d):
        return lax.rem(r + d, rows), c

    def at_col(peer):
        return r, peer

    barrier = pltpu.get_barrier_semaphore()
    for d in range(1, rows):
        pl.semaphore_signal(
            barrier, inc=1, device_id=at_row(d), device_id_type=pl.DeviceIdType.MESH
        )
    for d in range(1, peers):
        pl.semaphore_signal(
            barrier, inc=1, device_id=at_col(lax.rem(c + d, peers)),
            device_id_type=pl.DeviceIdType.MESH,
        )

    floated = features_ref[...].astype(F32)
    total = jnp.sum(floated * floated, axis=-1, keepdims=True)
    held[r] = (floated * lax.rsqrt(total + epsilon)).astype(BF)
    pl.semaphore_wait(barrier, rows + peers - 2)

    def remote(src, dst, send, recv, target):
        return pltpu.make_async_remote_copy(
            src_ref=src, dst_ref=dst, send_sem=send, recv_sem=recv, device_id=target,
            device_id_type=pl.DeviceIdType.MESH,
        )

    def strip(peer):
        return pl.ds(pl.multiple_of(peer * piece, piece), piece)

    here = strip(c)

    def slip(tile, d, target):
        return remote(
            held.at[tile, 0, 0], slips.at[tile], slip_send.at[tile, d], slip_recv.at[tile], target
        )

    for tile in range(2):
        @pl.when(r == tile)
        def _():
            for d in range(1, rows):
                slip(tile, d, at_row(d)).start()
            own = pltpu.make_async_copy(held.at[tile, 0, 0], slips.at[tile], keep_sem.at[0])
            own.start()
            own.wait()

    def up(step, owner, target):
        return remote(
            held.at[owner], held.at[owner], tall_send.at[0, step], tall_recv.at[0, step],
            (target, c),
        )

    def down(step, owner, target):
        return remote(
            held.at[owner], held.at[owner], tall_send.at[1, step], tall_recv.at[1, step],
            (target, c),
        )

    def hop(step):
        @pl.when((r + 1 < rows) & (r - step >= 0))
        def _():
            up(step, r - step, r + 1).start()

        @pl.when((r - 1 >= 0) & (r + step < rows))
        def _():
            down(step, r + step, r - 1).start()

    hop(0)

    for tile in range(2):
        @pl.when(r != tile)
        def _():
            slip(tile, 1, at_row(1)).wait_recv()

    def front_copy(d, owner, target):
        return remote(
            slips, front_ref.at[:, strip(owner)], front_send.at[d], front_recv.at[d], target
        )

    for d in range(1, peers):
        front_copy(d, c, at_col(lax.rem(c + d, peers))).start()
    kept = [
        pltpu.make_async_copy(slips, front_ref.at[:, here], keep_sem.at[0]),
        pltpu.make_async_copy(held.at[r], rows_ref.at[:, :, here], keep_sem.at[1]),
    ]
    for copy in kept:
        copy.start()

    def row_copy(d, owner, target):
        return remote(
            held.at[r], rows_ref.at[:, :, strip(owner)], row_send.at[d], row_recv.at[d], target
        )

    def pass_copy(d, owner, target):
        there = rows_ref.at[:, :, strip(owner)]
        return remote(there, there, pass_send.at[d], pass_recv.at[d], target)


    def col_copy(block, turn, owner, target):
        away = lax.rem(target - owner + peers, peers)
        return remote(
            held.at[block, :, turn], cols_ref.at[:, strip(owner)], col_send.at[away],
            col_recv.at[away], at_col(target),
        )

    def hand_out(block):
        for turn in range(stride):
            peer = block + turn * rows

            @pl.when(peer != c)
            def _():
                col_copy(block, turn, c, peer).start()

            @pl.when(peer == c)
            def _():
                pltpu.make_async_copy(
                    held.at[block, :, turn], cols_ref.at[:, here], keep_sem.at[2]
                ).start()

    def arrive(step):
        @pl.when(r - 1 - step >= 0)
        def _():
            up(step, r - 1 - step, r - 1).wait_recv()

        @pl.when(r + 1 + step < rows)
        def _():
            down(step, r + 1 + step, r + 1).wait_recv()

        if step + 2 < rows:
            hop(step + 1)

    def share(step):
        @pl.when(r - 1 - step >= 0)
        def _():
            hand_out(r - 1 - step)

        @pl.when(r + 1 + step < rows)
        def _():
            hand_out(r + 1 + step)

    arrive(0)
    share(0)
    for d in range(1, peers):
        front_copy(d, lax.rem(c - d + peers, peers), at_col(c)).wait_recv()
    kept[0].wait()
    row_copy(0, c, at_col(partner)).start()
    for d in range(1, pairs):
        row_copy(d, c, at_col(lax.rem(c + 2 * d, peers))).start()

    def pass_on():
        for d in range(1, pairs):
            owner = lax.rem(c - 2 * d + peers, peers)
            row_copy(d, owner, at_col(partner)).wait_recv()
            pass_copy(d, owner, at_col(partner)).start()

    blocks = 2 * tile_len // LEAF

    def between(at):
        step = at // 2 + 1
        if at % 2 and step < rows - 1:
            arrive(step)
            share(step)
        if at == blocks - 1:
            pass_on()

    front = front_ref[...].reshape(2 * tile_len, front_ref.shape[2])
    factor_steps(front, work, between)
    n = front.shape[0]
    for step in range(blocks // 2 + 1, rows - 1):
        arrive(step)
        share(step)
    hi, lo = split(work[:, n:2 * n])
    hi_ref[...] = hi
    lo_ref[...] = lo

    kept[1].wait()
    row_copy(0, partner, at_col(partner)).wait_recv()
    row_copy(0, c, at_col(partner)).wait_send()
    for d in range(1, pairs):
        owner = lax.rem(partner - 2 * d + peers, peers)
        pass_copy(d, owner, at_col(partner)).wait_recv()
        pass_copy(d, lax.rem(c - 2 * d + peers, peers), at_col(partner)).wait_send()
        row_copy(d, c, at_col(partner)).wait_send()

    def one_row(at):
        def step(turn):
            tile = at * stride + turn
            here = pl.ds(pl.multiple_of(tile * tile_len, tile_len), tile_len)

            def keep(first, second):
                fh, fl = split(first)
                panel_ref[here, :tile_len] = first
                panel_ref[here, tile_len:] = second
                p_ref[here, :tile_len] = fh
                p_ref[here, tile_len:n] = second.astype(BF)
                p_ref[here, n:n + LEAF] = fh[:, :LEAF]
                p_ref[here, n + LEAF:] = fl[:, :LEAF]

            return panel_steps(
                rows_ref[at, turn], tile * rows + r, front, hi_ref, lo_ref, keep
            )

        return step

    def row_panels(at, carry):
        together([one_row(at)(turn) for turn in range(stride)])
        return carry

    lax.fori_loop(0, rows_ref.shape[0], row_panels, 0)

    for d in range(1, peers):
        front_copy(d, c, at_col(partner)).wait_send()

    own_cols = pltpu.make_async_copy(rows_ref.at[:, c // rows], cols_ref, keep_sem.at[2])

    @pl.when(lax.rem(c, rows) == r)
    def _():
        own_cols.start()
        own_cols.wait()

    @pl.when(lax.rem(c, rows) != r)
    def _():
        pltpu.make_async_copy(held.at[0, :, 0], cols_ref.at[:, here], keep_sem.at[2]).wait()
        for d in range(1, peers):
            col_copy(0, 0, lax.rem(c - d + peers, peers), c).wait_recv()

    def one_column(b):
        here = slice(b * tile_len, (b + 1) * tile_len)

        def keep(first, second):
            fh, fl = split(first)
            q_ref[here, :tile_len] = fh
            q_ref[here, tile_len:n] = second.astype(BF)
            q_ref[here, n:n + LEAF] = fl[:, :LEAF]
            q_ref[here, n + LEAF:] = fh[:, :LEAF]

        return panel_steps(cols_ref[b], b * peers + c, front, hi_ref, lo_ref, keep)

    for b in range(0, cols_ref.shape[0], 2):
        together([one_column(i) for i in range(b, min(b + 2, cols_ref.shape[0]))])

    for d in range(1, peers):
        @pl.when(lax.rem(lax.rem(c + d, peers), rows) != r)
        def _():
            col_copy(0, 0, c, lax.rem(c + d, peers)).wait_send()
    for step in range(rows - 1):
        @pl.when((r + 1 < rows) & (r - step >= 0))
        def _():
            up(step, r, r + 1).wait_send()

        @pl.when((r - 1 >= 0) & (r + step < rows))
        def _():
            down(step, r, r - 1).wait_send()
    for tile in range(2):
        @pl.when(r == tile)
        def _():
            for d in range(1, rows):
                slip(tile, d, at_row(d)).wait_send()


def prepare(features, row_count, col_count):
    local_tiles, piece, feat = features.shape
    stride = col_count // row_count
    across = local_tiles // stride
    tile_len = piece * col_count
    n = 2 * tile_len
    dma = pltpu.SemaphoreType.DMA
    vmem = pl.BlockSpec(memory_space=pltpu.VMEM)
    rows = local_tiles * tile_len
    cols = across * tile_len
    return pl.pallas_call(
        prepare_body,
        out_shape=(
            jax.ShapeDtypeStruct((across, stride, tile_len, feat), BF),
            jax.ShapeDtypeStruct((across, tile_len, feat), BF),
            jax.ShapeDtypeStruct((rows, n), F32),
            jax.ShapeDtypeStruct((rows, n + 2 * LEAF), BF),
            jax.ShapeDtypeStruct((cols, n + 2 * LEAF), BF),
        ),
        in_specs=[vmem],
        out_specs=(vmem,) * 5,
        scratch_shapes=[
            pltpu.VMEM((row_count, across, stride, piece, feat), BF),
            pltpu.VMEM((2, piece, feat), BF),
            pltpu.VMEM((2, tile_len, feat), BF),
            pltpu.VMEM((n, n), BF),
            pltpu.VMEM((n, n), BF),
            pltpu.VMEM((n, 2 * n), F32),
            dma((2, row_count)), dma((2, row_count)), dma((2, row_count)), dma((2,)),
            dma((col_count,)), dma((col_count,)), dma((col_count,)), dma((col_count,)),
            dma((col_count,)), dma((col_count,)), dma((col_count,)), dma((col_count,)), dma((3,)),
        ],
        compiler_params=pltpu.CompilerParams(
            collective_id=0, has_side_effects=True, vmem_limit_bytes=28 * 2**20
        ),
        cost_estimate=pl.CostEstimate(flops=int(2e10), bytes_accessed=int(5e7), transcendentals=0),
        name="prepare",
    )(features.reshape(across, stride, piece, feat))


def schur_body(rows_ref, cols_ref, all_panels_ref, p_ref, q_ref, out_ref, panel_ref, panel_sem):
    own_row, own_col = lax.axis_index("row"), lax.axis_index("col")
    row_count, col_count = lax.axis_size("row"), lax.axis_size("col")
    across, tile_len = cols_ref.shape[0], cols_ref.shape[1]
    stride = rows_ref.shape[1]
    chunks = across * tile_len // LEAF
    per = tile_len // LEAF
    g = pl.program_id(0)
    out_panels = pltpu.make_async_copy(all_panels_ref, panel_ref, panel_sem)

    @pl.when(g == 0)
    def _():
        out_panels.start()

    size = stride * tile_len
    here = pl.ds(pl.multiple_of(g * size, size), size)
    points = rows_ref[g].reshape(size, rows_ref.shape[3])
    p = p_ref[here, :]
    for b in range(across):
        s = gram(points, cols_ref[b]) - dot(p, q_ref[b * tile_len:(b + 1) * tile_len, :], NT)
        for k in range(per):
            out_ref[pl.ds(b * per + k, size, stride=chunks), :] = s[:, k * LEAF:(k + 1) * LEAF]

    for turn in range(stride):
        tile_id = (g * stride + turn) * row_count + own_row
        for b in range(across):
            @pl.when(tile_id == b * col_count + own_col)
            def _():
                ident = eye(tile_len)
                for k in range(per):
                    at = pl.ds(turn * tile_len * chunks + b * per + k, tile_len, stride=chunks)
                    out_ref[at, :] = out_ref[at, :] + ident[:, k * LEAF:(k + 1) * LEAF]

    @pl.when(g == pl.num_programs(0) - 1)
    def _():
        out_panels.wait()


def schur(row_points, col_points, panels, p, q):
    across, stride, tile_len, _ = row_points.shape
    size = stride * tile_len
    chunks = across * tile_len // LEAF
    here = pl.BlockSpec(memory_space=pltpu.VMEM)
    return pl.pallas_call(
        schur_body,
        out_shape=(
            jax.ShapeDtypeStruct((across * size * chunks, LEAF), F32),
            jax.ShapeDtypeStruct(panels.shape, F32),
        ),
        grid=(across,),
        in_specs=[here] * 5,
        out_specs=(
            pl.BlockSpec((size * chunks, LEAF), lambda g: (g, 0)),
            pl.BlockSpec(memory_space=pl.ANY),
        ),
        scratch_shapes=[pltpu.SemaphoreType.DMA],
        compiler_params=pltpu.CompilerParams(
            dimension_semantics=("arbitrary",), vmem_limit_bytes=28 * 2**20
        ),
        name="schur",
    )(row_points, col_points, panels, p, q)


def per_device(features):
    row_count = lax.axis_size("row")
    col_count = lax.axis_size("col")
    local_tiles, _, piece, feat = features.shape
    tile_len = piece * col_count
    rows, cols, tall_panels, p, q = prepare(features[:, 0], row_count, col_count)
    big, panels = schur(rows, cols, tall_panels, p, q)
    across = cols.shape[0]
    return (
        big.reshape(local_tiles, 1, tile_len, across, 1, tile_len),
        panels.reshape(local_tiles, 1, tile_len, 2 * tile_len),
    )


def solution(mesh):
    return jax.shard_map(
        per_device,
        mesh=mesh,
        in_specs=(P(None, "row", "col", None),),
        out_specs=(P(None, "row", None, None, "col", None), P(None, "row", None, None)),
        check_vma=False,
    )
```

```python
import math

import jax
import jax.numpy as jnp
from jax import lax
from jax.experimental import pallas as pl
from jax.experimental.pallas import tpu as pltpu
from jax.sharding import PartitionSpec as P

kernel_gain = 2.0
epsilon = 1e-06
LEAF = 128
SUB = 16
gain2 = kernel_gain / math.log(2.0)
BF = jnp.bfloat16
F32 = jnp.float32
NT = (((1,), (1,)), ((), ()))
NN = (((1,), (0,)), ((), ()))
TN = (((0,), (0,)), ((), ()))


def split(x):
    hi = x.astype(BF)
    return hi, (x - hi.astype(F32)).astype(BF)


def dot(a, b, dims):
    return lax.dot_general(a, b, dims, preferred_element_type=F32)


def dot3(a, b, dims):
    ah, al = a
    bh, bl = b
    return dot(ah, bh, dims) + (dot(ah, bl, dims) + dot(al, bh, dims))


def gram(a, b):
    return jnp.exp2(gain2 * dot(a, b, NT) - gain2)


def eye(n):
    return (
        lax.broadcasted_iota(jnp.int32, (n, n), 0) == lax.broadcasted_iota(jnp.int32, (n, n), 1)
    ).astype(F32)


def half_leaf(block, sides):
    size = block.shape[0]
    groups = size // SUB
    x = [[m[g * SUB:(g + 1) * SUB] for g in range(groups)] for m in (block, *sides)]
    sub = lax.broadcasted_iota(jnp.int32, (SUB, LEAF), 0)

    def lane(v, at):
        return jnp.broadcast_to(v[:, at:at + 1], (SUB, LEAF))

    def row(v, at):
        return jnp.broadcast_to(v[at:at + 1, :], v.shape)

    for p in range(groups):
        c = [lane(x[0][p], p * SUB + k) for k in range(SUB)]
        pairs = []
        for j in range(0, SUB, 2):
            a, e, f = row(c[j], j), row(c[j], j + 1), row(c[j + 1], j + 1)
            r1, rd = lax.rsqrt(a), lax.rsqrt(a * f - e * e)
            across = e * r1
            r2 = a * r1 * rd
            l1 = c[j] * r1
            l2 = (c[j + 1] - l1 * across) * r2
            u1 = {k: row(l1, k) for k in range(j + 2, SUB)}
            u2 = {k: row(l2, k) for k in range(j + 2, SUB)}
            for k in range(j + 2, SUB):
                c[k] = c[k] - l1 * u1[k] - l2 * u2[k]
            b1 = jnp.where(sub > j + 1, l1, 0.0)
            b2 = jnp.where(sub > j + 1, l2, 0.0)
            w = []
            for m in x:
                w1 = row(m[p], j) * r1
                w2 = (row(m[p], j + 1) - w1 * across) * r2
                m[p] = jnp.where(
                    sub == j, w1, jnp.where(sub == j + 1, w2, m[p] - b1 * w1 - b2 * w2)
                )
                w.append((w1, w2))
            pairs.append((j, r1, across, r2, u1, u2, w))
        for g in range(p + 1, groups):
            c = [lane(x[0][g], p * SUB + k) for k in range(SUB)]
            for j, r1, across, r2, u1, u2, w in pairs:
                l1 = c[j] * r1
                l2 = (c[j + 1] - l1 * across) * r2
                for k in range(j + 2, SUB):
                    c[k] = c[k] - l1 * u1[k] - l2 * u2[k]
                for m, (w1, w2) in zip(x, w):
                    m[g] = m[g] - l1 * w1 - l2 * w2
    return [jnp.concatenate(m, axis=0) for m in x]


def leaf(block):
    h = LEAF // 2
    ident = eye(LEAF)
    upper, first = half_leaf(block[:h], [ident[:h]])
    right = jnp.where(lax.broadcasted_iota(jnp.int32, (h, LEAF), 1) >= h, upper, 0.0)
    rs = split(right)
    lower = block[h:] - dot3(rs, rs, TN)[h:]
    cross = dot3(rs, split(first), TN)[h:]
    packed = pltpu.roll(lower, h, 1)
    wide = lax.broadcasted_iota(jnp.int32, (h, LEAF), 1)
    packed = jnp.where(wide < h, packed, ident[:h][:, :])
    packed = jnp.where(wide < h, packed, pltpu.roll(ident[:h], h, 1))
    done = half_leaf(packed, [])[0]
    second = jnp.where(wide >= h, done, 0.0)
    inner = pltpu.roll(second, h, 1)
    low = second - dot3(split(inner), split(jnp.concatenate([cross, jnp.zeros_like(cross)], axis=0)), NN)
    return jnp.concatenate([first, low], axis=0)


def factor_steps(front, work, between):
    n = front.shape[0]
    blocks = n // LEAF
    spans = [slice(b * LEAF, (b + 1) * LEAF) for b in range(blocks)]
    m_spans = [slice(n + b * LEAF, n + (b + 1) * LEAF) for b in range(blocks)]
    for b in range(blocks):
        work[spans[b], b * LEAF:n] = gram(front[spans[b]], front[b * LEAF:])
    ident = eye(LEAF)
    block = work[spans[0], spans[0]] + ident
    for b in range(blocks):
        inverse = leaf(block)
        inv = split(inverse)
        work[spans[b], m_spans[b]] = inverse
        up = (b + 1) * LEAF
        if up < n:
            rs = split(dot3(inv, split(work[spans[b], up:n]), NN))
            rest = [tuple(v[:, i * LEAF:(i + 1) * LEAF] for v in rs) for i in range(blocks - b - 1)]
            block = work[spans[b + 1], spans[b + 1]] + ident - dot3(rest[0], rest[0], TN)
        between(b)
        if b:
            left = dot3(inv, split(work[spans[b], n:n + b * LEAF]), NN)
            work[spans[b], n:n + b * LEAF] = left
        if up < n:
            ms = split(work[spans[b], n:n + up])
            for i in range(b + 1, blocks):
                ri = rest[i - b - 1]
                at = i * LEAF
                if i > b + 1:
                    ahead = tuple(v[:, (i - b - 1) * LEAF:] for v in rs)
                    work[spans[i], at:n] = work[spans[i], at:n] - dot3(ri, ahead, TN)
                elif i + 1 < blocks:
                    ahead = tuple(v[:, LEAF:] for v in rs)
                    work[spans[i], at + LEAF:n] = work[spans[i], at + LEAF:n] - dot3(ri, ahead, TN)
                change = dot3(ri, ms, TN)
                if b:
                    old = slice(n, n + b * LEAF)
                    work[spans[i], old] = work[spans[i], old] - change[:, :b * LEAF]
                work[spans[i], m_spans[b]] = -change[:, b * LEAF:]
    for b in range(blocks):
        if b + 1 < blocks:
            work[spans[b], n + (b + 1) * LEAF:2 * n] = jnp.zeros((LEAF, n - (b + 1) * LEAF), F32)


def panel_steps(points, tile_id, front, hi_ref, lo_ref, keep):
    t = points.shape[0]
    values = gram(points, front)
    at = lax.broadcasted_iota(jnp.int32, values.shape, 0) + tile_id * t
    values = values + (at == lax.broadcasted_iota(jnp.int32, values.shape, 1)).astype(F32)
    hi, lo = split(values)
    yield
    first = dot3((hi[:, :t], lo[:, :t]), (hi_ref[:t, :t], lo_ref[:t, :t]), NT)
    yield
    second = dot3((hi, lo), (hi_ref[t:, :], lo_ref[t:, :]), NT)
    yield
    keep(first, second)
    yield


def together(steps):
    for _ in zip(*steps):
        pass


def prepare_body(
    features_ref, rows_ref, cols_ref, panel_ref, p_ref, q_ref, held, slips, front_ref, hi_ref,
    lo_ref, work, tall_send,
    tall_recv, slip_send, slip_recv, front_send, front_recv, row_send, row_recv, pass_send,
    pass_recv, col_send, col_recv, keep_sem,
):
    rows = lax.axis_size("row")
    peers = lax.axis_size("col")
    r = lax.axis_index("row")
    c = lax.axis_index("col")
    stride, piece = features_ref.shape[1], features_ref.shape[2]
    tile_len = piece * peers
    pairs = peers // 2
    partner = c + 1 - 2 * lax.rem(c, 2)

    def at_row(d):
        return lax.rem(r + d, rows), c

    def at_col(peer):
        return r, peer

    barrier = pltpu.get_barrier_semaphore()
    for d in range(1, rows):
        pl.semaphore_signal(
            barrier, inc=1, device_id=at_row(d), device_id_type=pl.DeviceIdType.MESH
        )
    for d in range(1, peers):
        pl.semaphore_signal(
            barrier, inc=1, device_id=at_col(lax.rem(c + d, peers)),
            device_id_type=pl.DeviceIdType.MESH,
        )

    floated = features_ref[...].astype(F32)
    total = jnp.sum(floated * floated, axis=-1, keepdims=True)
    held[r] = (floated * lax.rsqrt(total + epsilon)).astype(BF)
    pl.semaphore_wait(barrier, rows + peers - 2)

    def remote(src, dst, send, recv, target):
        return pltpu.make_async_remote_copy(
            src_ref=src, dst_ref=dst, send_sem=send, recv_sem=recv, device_id=target,
            device_id_type=pl.DeviceIdType.MESH,
        )

    def strip(peer):
        return pl.ds(pl.multiple_of(peer * piece, piece), piece)

    here = strip(c)

    def slip(tile, d, target):
        return remote(
            held.at[tile, 0, 0], slips.at[tile], slip_send.at[tile, d], slip_recv.at[tile], target
        )

    for tile in range(2):
        @pl.when(r == tile)
        def _():
            for d in range(1, rows):
                slip(tile, d, at_row(d)).start()
            own = pltpu.make_async_copy(held.at[tile, 0, 0], slips.at[tile], keep_sem.at[0])
            own.start()
            own.wait()

    def up(step, owner, target):
        return remote(
            held.at[owner], held.at[owner], tall_send.at[0, step], tall_recv.at[0, step],
            (target, c),
        )

    def down(step, owner, target):
        return remote(
            held.at[owner], held.at[owner], tall_send.at[1, step], tall_recv.at[1, step],
            (target, c),
        )

    def hop(step):
        @pl.when((r + 1 < rows) & (r - step >= 0))
        def _():
            up(step, r - step, r + 1).start()

        @pl.when((r - 1 >= 0) & (r + step < rows))
        def _():
            down(step, r + step, r - 1).start()

    hop(0)

    for tile in range(2):
        @pl.when(r != tile)
        def _():
            slip(tile, 1, at_row(1)).wait_recv()

    def front_copy(d, owner, target):
        return remote(
            slips, front_ref.at[:, strip(owner)], front_send.at[d], front_recv.at[d], target
        )

    for d in range(1, peers):
        front_copy(d, c, at_col(lax.rem(c + d, peers))).start()
    kept = [
        pltpu.make_async_copy(slips, front_ref.at[:, here], keep_sem.at[0]),
        pltpu.make_async_copy(held.at[r], rows_ref.at[:, :, here], keep_sem.at[1]),
    ]
    for copy in kept:
        copy.start()

    def row_copy(d, owner, target):
        return remote(
            held.at[r], rows_ref.at[:, :, strip(owner)], row_send.at[d], row_recv.at[d], target
        )

    def pass_copy(d, owner, target):
        there = rows_ref.at[:, :, strip(owner)]
        return remote(there, there, pass_send.at[d], pass_recv.at[d], target)


    def col_copy(block, turn, owner, target):
        away = lax.rem(target - owner + peers, peers)
        return remote(
            held.at[block, :, turn], cols_ref.at[:, strip(owner)], col_send.at[away],
            col_recv.at[away], at_col(target),
        )

    def hand_out(block):
        for turn in range(stride):
            peer = block + turn * rows

            @pl.when(peer != c)
            def _():
                col_copy(block, turn, c, peer).start()

            @pl.when(peer == c)
            def _():
                pltpu.make_async_copy(
                    held.at[block, :, turn], cols_ref.at[:, here], keep_sem.at[2]
                ).start()

    def arrive(step):
        @pl.when(r - 1 - step >= 0)
        def _():
            up(step, r - 1 - step, r - 1).wait_recv()

        @pl.when(r + 1 + step < rows)
        def _():
            down(step, r + 1 + step, r + 1).wait_recv()

        if step + 2 < rows:
            hop(step + 1)

    def share(step):
        @pl.when(r - 1 - step >= 0)
        def _():
            hand_out(r - 1 - step)

        @pl.when(r + 1 + step < rows)
        def _():
            hand_out(r + 1 + step)

    arrive(0)
    share(0)
    for d in range(1, peers):
        front_copy(d, lax.rem(c - d + peers, peers), at_col(c)).wait_recv()
    kept[0].wait()
    row_copy(0, c, at_col(partner)).start()
    for d in range(1, pairs):
        row_copy(d, c, at_col(lax.rem(c + 2 * d, peers))).start()

    def pass_on():
        for d in range(1, pairs):
            owner = lax.rem(c - 2 * d + peers, peers)
            row_copy(d, owner, at_col(partner)).wait_recv()
            pass_copy(d, owner, at_col(partner)).start()

    blocks = 2 * tile_len // LEAF

    def between(at):
        step = at // 2 + 1
        if at % 2 and step < rows - 1:
            arrive(step)
            share(step)
        if at == blocks - 1:
            pass_on()

    front = front_ref[...].reshape(2 * tile_len, front_ref.shape[2])
    factor_steps(front, work, between)
    n = front.shape[0]
    for step in range(blocks // 2 + 1, rows - 1):
        arrive(step)
        share(step)
    hi, lo = split(work[:, n:2 * n])
    hi_ref[...] = hi
    lo_ref[...] = lo

    kept[1].wait()
    row_copy(0, partner, at_col(partner)).wait_recv()
    row_copy(0, c, at_col(partner)).wait_send()
    for d in range(1, pairs):
        owner = lax.rem(partner - 2 * d + peers, peers)
        pass_copy(d, owner, at_col(partner)).wait_recv()
        pass_copy(d, lax.rem(c - 2 * d + peers, peers), at_col(partner)).wait_send()
        row_copy(d, c, at_col(partner)).wait_send()

    def one_row(at):
        def step(turn):
            tile = at * stride + turn
            here = pl.ds(pl.multiple_of(tile * tile_len, tile_len), tile_len)

            def keep(first, second):
                fh, fl = split(first)
                panel_ref[here, :tile_len] = first
                panel_ref[here, tile_len:] = second
                p_ref[here, :tile_len] = fh
                p_ref[here, tile_len:n] = second.astype(BF)
                p_ref[here, n:n + LEAF] = fh[:, :LEAF]
                p_ref[here, n + LEAF:] = fl[:, :LEAF]

            return panel_steps(
                rows_ref[at, turn], tile * rows + r, front, hi_ref, lo_ref, keep
            )

        return step

    def row_panels(at, carry):
        together(
            [one_row(at * deep + k)(turn) for k in range(deep) for turn in range(stride)]
        )
        return carry

    deep = math.gcd(rows_ref.shape[0], 6)
    lax.fori_loop(0, rows_ref.shape[0] // deep, row_panels, 0)

    for d in range(1, peers):
        front_copy(d, c, at_col(partner)).wait_send()

    own_cols = pltpu.make_async_copy(rows_ref.at[:, c // rows], cols_ref, keep_sem.at[2])

    @pl.when(lax.rem(c, rows) == r)
    def _():
        own_cols.start()
        own_cols.wait()

    @pl.when(lax.rem(c, rows) != r)
    def _():
        pltpu.make_async_copy(held.at[0, :, 0], cols_ref.at[:, here], keep_sem.at[2]).wait()
        for d in range(1, peers):
            col_copy(0, 0, lax.rem(c - d + peers, peers), c).wait_recv()

    def one_column(b):
        here = slice(b * tile_len, (b + 1) * tile_len)

        def keep(first, second):
            fh, fl = split(first)
            q_ref[here, :tile_len] = fh
            q_ref[here, tile_len:n] = second.astype(BF)
            q_ref[here, n:n + LEAF] = fl[:, :LEAF]
            q_ref[here, n + LEAF:] = fh[:, :LEAF]

        return panel_steps(cols_ref[b], b * peers + c, front, hi_ref, lo_ref, keep)

    together([one_column(b) for b in range(cols_ref.shape[0])])

    for d in range(1, peers):
        @pl.when(lax.rem(lax.rem(c + d, peers), rows) != r)
        def _():
            col_copy(0, 0, c, lax.rem(c + d, peers)).wait_send()
    for step in range(rows - 1):
        @pl.when((r + 1 < rows) & (r - step >= 0))
        def _():
            up(step, r, r + 1).wait_send()

        @pl.when((r - 1 >= 0) & (r + step < rows))
        def _():
            down(step, r, r - 1).wait_send()
    for tile in range(2):
        @pl.when(r == tile)
        def _():
            for d in range(1, rows):
                slip(tile, d, at_row(d)).wait_send()


def prepare(features, row_count, col_count):
    local_tiles, piece, feat = features.shape
    stride = col_count // row_count
    across = local_tiles // stride
    tile_len = piece * col_count
    n = 2 * tile_len
    dma = pltpu.SemaphoreType.DMA
    vmem = pl.BlockSpec(memory_space=pltpu.VMEM)
    rows = local_tiles * tile_len
    cols = across * tile_len
    return pl.pallas_call(
        prepare_body,
        out_shape=(
            jax.ShapeDtypeStruct((across, stride, tile_len, feat), BF),
            jax.ShapeDtypeStruct((across, tile_len, feat), BF),
            jax.ShapeDtypeStruct((rows, n), F32),
            jax.ShapeDtypeStruct((rows, n + 2 * LEAF), BF),
            jax.ShapeDtypeStruct((cols, n + 2 * LEAF), BF),
        ),
        in_specs=[vmem],
        out_specs=(vmem,) * 5,
        scratch_shapes=[
            pltpu.VMEM((row_count, across, stride, piece, feat), BF),
            pltpu.VMEM((2, piece, feat), BF),
            pltpu.VMEM((2, tile_len, feat), BF),
            pltpu.VMEM((n, n), BF),
            pltpu.VMEM((n, n), BF),
            pltpu.VMEM((n, 2 * n), F32),
            dma((2, row_count)), dma((2, row_count)), dma((2, row_count)), dma((2,)),
            dma((col_count,)), dma((col_count,)), dma((col_count,)), dma((col_count,)),
            dma((col_count,)), dma((col_count,)), dma((col_count,)), dma((col_count,)), dma((3,)),
        ],
        compiler_params=pltpu.CompilerParams(
            collective_id=0, has_side_effects=True, vmem_limit_bytes=38 * 2**20
        ),
        cost_estimate=pl.CostEstimate(flops=int(2e10), bytes_accessed=int(5e7), transcendentals=0),
        name="prepare",
    )(features.reshape(across, stride, piece, feat))


def schur_body(
    row_ref, col_ref, rows_ref, cols_ref, all_panels_ref, p_ref, q_ref, out_ref, panel_ref,
    panel_sem,
):
    own_row, own_col = row_ref[0], col_ref[0]
    row_count, col_count = lax.axis_size("row"), lax.axis_size("col")
    across, tile_len = cols_ref.shape[0], cols_ref.shape[1]
    stride = rows_ref.shape[1]
    chunks = across * tile_len // LEAF
    per = tile_len // LEAF
    g = pl.program_id(0)
    out_panels = pltpu.make_async_copy(all_panels_ref, panel_ref, panel_sem)

    @pl.when(g == 0)
    def _():
        out_panels.start()

    size = stride * tile_len
    here = pl.ds(pl.multiple_of(g * size, size), size)
    points = rows_ref[g].reshape(size, rows_ref.shape[3])
    p = p_ref[here, :]
    for b in range(across):
        s = gram(points, cols_ref[b]) - dot(p, q_ref[b * tile_len:(b + 1) * tile_len, :], NT)
        for k in range(per):
            out_ref[pl.ds(b * per + k, size, stride=chunks), :] = s[:, k * LEAF:(k + 1) * LEAF]

    for turn in range(stride):
        tile_id = (g * stride + turn) * row_count + own_row
        for b in range(across):
            @pl.when(tile_id == b * col_count + own_col)
            def _():
                ident = eye(tile_len)
                for k in range(per):
                    at = pl.ds(turn * tile_len * chunks + b * per + k, tile_len, stride=chunks)
                    out_ref[at, :] = out_ref[at, :] + ident[:, k * LEAF:(k + 1) * LEAF]

    @pl.when(g == pl.num_programs(0) - 1)
    def _():
        out_panels.wait()


def schur(own_row, own_col, row_points, col_points, panels, p, q):
    across, stride, tile_len, _ = row_points.shape
    size = stride * tile_len
    chunks = across * tile_len // LEAF
    here = pl.BlockSpec(memory_space=pltpu.VMEM)
    scalar = pl.BlockSpec(memory_space=pltpu.SMEM)
    return pl.pallas_call(
        schur_body,
        out_shape=(
            jax.ShapeDtypeStruct((across * size * chunks, LEAF), F32),
            jax.ShapeDtypeStruct(panels.shape, F32),
        ),
        grid=(across,),
        in_specs=[scalar] * 2 + [here] * 5,
        out_specs=(
            pl.BlockSpec((size * chunks, LEAF), lambda g: (g, 0)),
            pl.BlockSpec(memory_space=pl.ANY),
        ),
        scratch_shapes=[pltpu.SemaphoreType.DMA],
        compiler_params=pltpu.CompilerParams(
            dimension_semantics=("arbitrary",), vmem_limit_bytes=28 * 2**20
        ),
        name="schur",
    )(own_row.reshape(1), own_col.reshape(1), row_points, col_points, panels, p, q)


def per_device(features):
    row_count = lax.axis_size("row")
    col_count = lax.axis_size("col")
    local_tiles, _, piece, feat = features.shape
    tile_len = piece * col_count
    rows, cols, tall_panels, p, q = prepare(features[:, 0], row_count, col_count)
    big, panels = schur(
        lax.axis_index("row"), lax.axis_index("col"), rows, cols, tall_panels, p, q
    )
    across = cols.shape[0]
    return (
        big.reshape(local_tiles, 1, tile_len, across, 1, tile_len),
        panels.reshape(local_tiles, 1, tile_len, 2 * tile_len),
    )


def solution(mesh):
    return jax.shard_map(
        per_device,
        mesh=mesh,
        in_specs=(P(None, "row", "col", None),),
        out_specs=(P(None, "row", None, None, "col", None), P(None, "row", None, None)),
        check_vma=False,
    )
```

```python
import math

import jax
import jax.numpy as jnp
from jax import lax
from jax.experimental import pallas as pl
from jax.experimental.pallas import tpu as pltpu
from jax.sharding import PartitionSpec as P

kernel_gain = 2.0
epsilon = 1e-06
LEAF = 128
SUB = 16
gain2 = kernel_gain / math.log(2.0)
BF = jnp.bfloat16
F32 = jnp.float32
NT = (((1,), (1,)), ((), ()))
NN = (((1,), (0,)), ((), ()))
TN = (((0,), (0,)), ((), ()))


def split(x):
    hi = x.astype(BF)
    return hi, (x - hi.astype(F32)).astype(BF)


def dot(a, b, dims):
    return lax.dot_general(a, b, dims, preferred_element_type=F32)


def dot3(a, b, dims):
    ah, al = a
    bh, bl = b
    return dot(ah, bh, dims) + (dot(ah, bl, dims) + dot(al, bh, dims))


def gram(a, b):
    return jnp.exp2(gain2 * dot(a, b, NT) - gain2)


def eye(n):
    return (
        lax.broadcasted_iota(jnp.int32, (n, n), 0) == lax.broadcasted_iota(jnp.int32, (n, n), 1)
    ).astype(F32)


def half_leaf(block, sides):
    size = block.shape[0]
    groups = size // SUB
    x = [[m[g * SUB:(g + 1) * SUB] for g in range(groups)] for m in (block, *sides)]
    sub = lax.broadcasted_iota(jnp.int32, (SUB, LEAF), 0)

    def lane(v, at):
        return jnp.broadcast_to(v[:, at:at + 1], (SUB, LEAF))

    def row(v, at):
        return jnp.broadcast_to(v[at:at + 1, :], v.shape)

    for p in range(groups):
        c = [lane(x[0][p], p * SUB + k) for k in range(SUB)]
        pairs = []
        for j in range(0, SUB, 2):
            a, e, f = row(c[j], j), row(c[j], j + 1), row(c[j + 1], j + 1)
            r1, rd = lax.rsqrt(a), lax.rsqrt(a * f - e * e)
            across = e * r1
            r2 = a * r1 * rd
            l1 = c[j] * r1
            l2 = (c[j + 1] - l1 * across) * r2
            u1 = {k: row(l1, k) for k in range(j + 2, SUB)}
            u2 = {k: row(l2, k) for k in range(j + 2, SUB)}
            for k in range(j + 2, SUB):
                c[k] = c[k] - l1 * u1[k] - l2 * u2[k]
            b1 = jnp.where(sub > j + 1, l1, 0.0)
            b2 = jnp.where(sub > j + 1, l2, 0.0)
            w = []
            for m in x:
                w1 = row(m[p], j) * r1
                w2 = (row(m[p], j + 1) - w1 * across) * r2
                m[p] = jnp.where(
                    sub == j, w1, jnp.where(sub == j + 1, w2, m[p] - b1 * w1 - b2 * w2)
                )
                w.append((w1, w2))
            pairs.append((j, r1, across, r2, u1, u2, w))
        for g in range(p + 1, groups):
            c = [lane(x[0][g], p * SUB + k) for k in range(SUB)]
            for j, r1, across, r2, u1, u2, w in pairs:
                l1 = c[j] * r1
                l2 = (c[j + 1] - l1 * across) * r2
                for k in range(j + 2, SUB):
                    c[k] = c[k] - l1 * u1[k] - l2 * u2[k]
                for m, (w1, w2) in zip(x, w):
                    m[g] = m[g] - l1 * w1 - l2 * w2
    return [jnp.concatenate(m, axis=0) for m in x]


def leaf(block, rest=None):
    h = LEAF // 2
    ident = eye(LEAF)
    upper, first = half_leaf(block[:h], [ident[:h]])
    right = jnp.where(lax.broadcasted_iota(jnp.int32, (h, LEAF), 1) >= h, upper, 0.0)
    rs = split(right)
    lower = block[h:] - dot3(rs, rs, TN)[h:]
    fs = split(first)
    cross = dot3(rs, fs, TN)[h:]
    if rest is not None:
        top = dot3(fs, split(rest), NN)
        pre = rest[h:] - dot3(rs, split(top), TN)[h:]
    packed = pltpu.roll(lower, h, 1)
    wide = lax.broadcasted_iota(jnp.int32, (h, LEAF), 1)
    packed = jnp.where(wide < h, packed, ident[:h][:, :])
    packed = jnp.where(wide < h, packed, pltpu.roll(ident[:h], h, 1))
    done = half_leaf(packed, [])[0]
    second = jnp.where(wide >= h, done, 0.0)
    inner = pltpu.roll(second, h, 1)
    inner = split(inner)
    low = second - dot3(inner, split(jnp.concatenate([cross, jnp.zeros_like(cross)], axis=0)), NN)
    inverse = jnp.concatenate([first, low], axis=0)
    if rest is None:
        return inverse, None
    bottom = dot3(inner, split(jnp.concatenate([pre, jnp.zeros_like(pre)], axis=0)), NN)
    return inverse, jnp.concatenate([top, bottom], axis=0)


def factor_steps(front, work, between):
    n = front.shape[0]
    blocks = n // LEAF
    spans = [slice(b * LEAF, (b + 1) * LEAF) for b in range(blocks)]
    m_spans = [slice(n + b * LEAF, n + (b + 1) * LEAF) for b in range(blocks)]
    for b in range(blocks):
        work[spans[b], b * LEAF:n] = gram(front[spans[b]], front[b * LEAF:])
    ident = eye(LEAF)
    block = work[spans[0], spans[0]] + ident
    for b in range(blocks):
        up = (b + 1) * LEAF
        inverse, right = leaf(block, work[spans[b], up:n] if up < n else None)
        inv = split(inverse)
        work[spans[b], m_spans[b]] = inverse
        if up < n:
            rs = split(right)
            rest = [tuple(v[:, i * LEAF:(i + 1) * LEAF] for v in rs) for i in range(blocks - b - 1)]
            block = work[spans[b + 1], spans[b + 1]] + ident - dot3(rest[0], rest[0], TN)
        between(b)
        if b:
            left = dot3(inv, split(work[spans[b], n:n + b * LEAF]), NN)
            work[spans[b], n:n + b * LEAF] = left
        if up < n:
            ms = split(work[spans[b], n:n + up])
            for i in range(b + 1, blocks):
                ri = rest[i - b - 1]
                at = i * LEAF
                if i > b + 1:
                    ahead = tuple(v[:, (i - b - 1) * LEAF:] for v in rs)
                    work[spans[i], at:n] = work[spans[i], at:n] - dot3(ri, ahead, TN)
                elif i + 1 < blocks:
                    ahead = tuple(v[:, LEAF:] for v in rs)
                    work[spans[i], at + LEAF:n] = work[spans[i], at + LEAF:n] - dot3(ri, ahead, TN)
                change = dot3(ri, ms, TN)
                if b:
                    old = slice(n, n + b * LEAF)
                    work[spans[i], old] = work[spans[i], old] - change[:, :b * LEAF]
                work[spans[i], m_spans[b]] = -change[:, b * LEAF:]
    for b in range(blocks):
        if b + 1 < blocks:
            work[spans[b], n + (b + 1) * LEAF:2 * n] = jnp.zeros((LEAF, n - (b + 1) * LEAF), F32)


def panel_steps(points, tile_id, front, hi_ref, lo_ref, keep):
    t = points.shape[0]
    values = gram(points, front)
    at = lax.broadcasted_iota(jnp.int32, values.shape, 0) + tile_id * t
    values = values + (at == lax.broadcasted_iota(jnp.int32, values.shape, 1)).astype(F32)
    hi, lo = split(values)
    yield
    first = dot3((hi[:, :t], lo[:, :t]), (hi_ref[:t, :t], lo_ref[:t, :t]), NT)
    yield
    second = dot3((hi, lo), (hi_ref[t:, :], lo_ref[t:, :]), NT)
    yield
    keep(first, second)
    yield


def together(steps):
    for _ in zip(*steps):
        pass


def prepare_body(
    features_ref, rows_ref, cols_ref, panel_ref, p_ref, q_ref, held, slips, front_ref, hi_ref,
    lo_ref, work, tall_send,
    tall_recv, slip_send, slip_recv, front_send, front_recv, row_send, row_recv, pass_send,
    pass_recv, col_send, col_recv, keep_sem,
):
    rows = lax.axis_size("row")
    peers = lax.axis_size("col")
    r = lax.axis_index("row")
    c = lax.axis_index("col")
    stride, piece = features_ref.shape[1], features_ref.shape[2]
    tile_len = piece * peers
    pairs = peers // 2
    partner = c + 1 - 2 * lax.rem(c, 2)

    def at_row(d):
        return lax.rem(r + d, rows), c

    def at_col(peer):
        return r, peer

    barrier = pltpu.get_barrier_semaphore()
    for d in range(1, rows):
        pl.semaphore_signal(
            barrier, inc=1, device_id=at_row(d), device_id_type=pl.DeviceIdType.MESH
        )
    for d in range(1, peers):
        pl.semaphore_signal(
            barrier, inc=1, device_id=at_col(lax.rem(c + d, peers)),
            device_id_type=pl.DeviceIdType.MESH,
        )

    floated = features_ref[...].astype(F32)
    total = jnp.sum(floated * floated, axis=-1, keepdims=True)
    held[r] = (floated * lax.rsqrt(total + epsilon)).astype(BF)
    pl.semaphore_wait(barrier, rows + peers - 2)

    def remote(src, dst, send, recv, target):
        return pltpu.make_async_remote_copy(
            src_ref=src, dst_ref=dst, send_sem=send, recv_sem=recv, device_id=target,
            device_id_type=pl.DeviceIdType.MESH,
        )

    def strip(peer):
        return pl.ds(pl.multiple_of(peer * piece, piece), piece)

    here = strip(c)

    def slip(tile, d, target):
        return remote(
            held.at[tile, 0, 0], slips.at[tile], slip_send.at[tile, d], slip_recv.at[tile], target
        )

    for tile in range(2):
        @pl.when(r == tile)
        def _():
            for d in range(1, rows):
                slip(tile, d, at_row(d)).start()
            own = pltpu.make_async_copy(held.at[tile, 0, 0], slips.at[tile], keep_sem.at[0])
            own.start()
            own.wait()

    def up(step, owner, target):
        return remote(
            held.at[owner], held.at[owner], tall_send.at[0, step], tall_recv.at[0, step],
            (target, c),
        )

    def down(step, owner, target):
        return remote(
            held.at[owner], held.at[owner], tall_send.at[1, step], tall_recv.at[1, step],
            (target, c),
        )

    def hop(step):
        @pl.when((r + 1 < rows) & (r - step >= 0))
        def _():
            up(step, r - step, r + 1).start()

        @pl.when((r - 1 >= 0) & (r + step < rows))
        def _():
            down(step, r + step, r - 1).start()

    hop(0)

    for tile in range(2):
        @pl.when(r != tile)
        def _():
            slip(tile, 1, at_row(1)).wait_recv()

    def front_copy(d, owner, target):
        return remote(
            slips, front_ref.at[:, strip(owner)], front_send.at[d], front_recv.at[d], target
        )

    for d in range(1, peers):
        front_copy(d, c, at_col(lax.rem(c + d, peers))).start()
    kept = [
        pltpu.make_async_copy(slips, front_ref.at[:, here], keep_sem.at[0]),
        pltpu.make_async_copy(held.at[r], rows_ref.at[:, :, here], keep_sem.at[1]),
    ]
    for copy in kept:
        copy.start()

    def row_copy(d, owner, target):
        return remote(
            held.at[r], rows_ref.at[:, :, strip(owner)], row_send.at[d], row_recv.at[d], target
        )

    def pass_copy(d, owner, target):
        there = rows_ref.at[:, :, strip(owner)]
        return remote(there, there, pass_send.at[d], pass_recv.at[d], target)


    def col_copy(block, turn, owner, target):
        away = lax.rem(target - owner + peers, peers)
        return remote(
            held.at[block, :, turn], cols_ref.at[:, strip(owner)], col_send.at[away],
            col_recv.at[away], at_col(target),
        )

    def hand_out(block):
        for turn in range(stride):
            peer = block + turn * rows

            @pl.when(peer != c)
            def _():
                col_copy(block, turn, c, peer).start()

            @pl.when(peer == c)
            def _():
                pltpu.make_async_copy(
                    held.at[block, :, turn], cols_ref.at[:, here], keep_sem.at[2]
                ).start()

    def arrive(step):
        @pl.when(r - 1 - step >= 0)
        def _():
            up(step, r - 1 - step, r - 1).wait_recv()

        @pl.when(r + 1 + step < rows)
        def _():
            down(step, r + 1 + step, r + 1).wait_recv()

        if step + 2 < rows:
            hop(step + 1)

    def share(step):
        @pl.when(r - 1 - step >= 0)
        def _():
            hand_out(r - 1 - step)

        @pl.when(r + 1 + step < rows)
        def _():
            hand_out(r + 1 + step)

    arrive(0)
    share(0)
    for d in range(1, peers):
        front_copy(d, lax.rem(c - d + peers, peers), at_col(c)).wait_recv()
    kept[0].wait()
    row_copy(0, c, at_col(partner)).start()
    for d in range(1, pairs):
        row_copy(d, c, at_col(lax.rem(c + 2 * d, peers))).start()

    def pass_on():
        for d in range(1, pairs):
            owner = lax.rem(c - 2 * d + peers, peers)
            row_copy(d, owner, at_col(partner)).wait_recv()
            pass_copy(d, owner, at_col(partner)).start()

    blocks = 2 * tile_len // LEAF

    def between(at):
        step = at // 2 + 1
        if at % 2 and step < rows - 1:
            arrive(step)
            share(step)
        if at == blocks - 1:
            pass_on()

    front = front_ref[...].reshape(2 * tile_len, front_ref.shape[2])
    factor_steps(front, work, between)
    n = front.shape[0]
    for step in range(blocks // 2 + 1, rows - 1):
        arrive(step)
        share(step)
    hi, lo = split(work[:, n:2 * n])
    hi_ref[...] = hi
    lo_ref[...] = lo

    kept[1].wait()
    row_copy(0, partner, at_col(partner)).wait_recv()
    row_copy(0, c, at_col(partner)).wait_send()
    for d in range(1, pairs):
        owner = lax.rem(partner - 2 * d + peers, peers)
        pass_copy(d, owner, at_col(partner)).wait_recv()
        pass_copy(d, lax.rem(c - 2 * d + peers, peers), at_col(partner)).wait_send()
        row_copy(d, c, at_col(partner)).wait_send()

    def one_row(at):
        def step(turn):
            tile = at * stride + turn
            here = pl.ds(pl.multiple_of(tile * tile_len, tile_len), tile_len)

            def keep(first, second):
                fh, fl = split(first)
                panel_ref[here, :tile_len] = first
                panel_ref[here, tile_len:] = second
                p_ref[here, :tile_len] = fh
                p_ref[here, tile_len:n] = second.astype(BF)
                p_ref[here, n:n + LEAF] = fh[:, :LEAF]
                p_ref[here, n + LEAF:] = fl[:, :LEAF]

            return panel_steps(
                rows_ref[at, turn], tile * rows + r, front, hi_ref, lo_ref, keep
            )

        return step

    def row_panels(at, carry):
        together(
            [one_row(at * deep + k)(turn) for k in range(deep) for turn in range(stride)]
        )
        return carry

    deep = math.gcd(rows_ref.shape[0], 6)
    lax.fori_loop(0, rows_ref.shape[0] // deep, row_panels, 0)

    for d in range(1, peers):
        front_copy(d, c, at_col(partner)).wait_send()

    own_cols = pltpu.make_async_copy(rows_ref.at[:, c // rows], cols_ref, keep_sem.at[2])

    @pl.when(lax.rem(c, rows) == r)
    def _():
        own_cols.start()
        own_cols.wait()

    @pl.when(lax.rem(c, rows) != r)
    def _():
        pltpu.make_async_copy(held.at[0, :, 0], cols_ref.at[:, here], keep_sem.at[2]).wait()
        for d in range(1, peers):
            col_copy(0, 0, lax.rem(c - d + peers, peers), c).wait_recv()

    def one_column(b):
        here = slice(b * tile_len, (b + 1) * tile_len)

        def keep(first, second):
            fh, fl = split(first)
            q_ref[here, :tile_len] = fh
            q_ref[here, tile_len:n] = second.astype(BF)
            q_ref[here, n:n + LEAF] = fl[:, :LEAF]
            q_ref[here, n + LEAF:] = fh[:, :LEAF]

        return panel_steps(cols_ref[b], b * peers + c, front, hi_ref, lo_ref, keep)

    together([one_column(b) for b in range(cols_ref.shape[0])])

    for d in range(1, peers):
        @pl.when(lax.rem(lax.rem(c + d, peers), rows) != r)
        def _():
            col_copy(0, 0, c, lax.rem(c + d, peers)).wait_send()
    for step in range(rows - 1):
        @pl.when((r + 1 < rows) & (r - step >= 0))
        def _():
            up(step, r, r + 1).wait_send()

        @pl.when((r - 1 >= 0) & (r + step < rows))
        def _():
            down(step, r, r - 1).wait_send()
    for tile in range(2):
        @pl.when(r == tile)
        def _():
            for d in range(1, rows):
                slip(tile, d, at_row(d)).wait_send()


def prepare(features, row_count, col_count):
    local_tiles, piece, feat = features.shape
    stride = col_count // row_count
    across = local_tiles // stride
    tile_len = piece * col_count
    n = 2 * tile_len
    dma = pltpu.SemaphoreType.DMA
    vmem = pl.BlockSpec(memory_space=pltpu.VMEM)
    rows = local_tiles * tile_len
    cols = across * tile_len
    return pl.pallas_call(
        prepare_body,
        out_shape=(
            jax.ShapeDtypeStruct((across, stride, tile_len, feat), BF),
            jax.ShapeDtypeStruct((across, tile_len, feat), BF),
            jax.ShapeDtypeStruct((rows, n), F32),
            jax.ShapeDtypeStruct((rows, n + 2 * LEAF), BF),
            jax.ShapeDtypeStruct((cols, n + 2 * LEAF), BF),
        ),
        in_specs=[vmem],
        out_specs=(vmem,) * 5,
        scratch_shapes=[
            pltpu.VMEM((row_count, across, stride, piece, feat), BF),
            pltpu.VMEM((2, piece, feat), BF),
            pltpu.VMEM((2, tile_len, feat), BF),
            pltpu.VMEM((n, n), BF),
            pltpu.VMEM((n, n), BF),
            pltpu.VMEM((n, 2 * n), F32),
            dma((2, row_count)), dma((2, row_count)), dma((2, row_count)), dma((2,)),
            dma((col_count,)), dma((col_count,)), dma((col_count,)), dma((col_count,)),
            dma((col_count,)), dma((col_count,)), dma((col_count,)), dma((col_count,)), dma((3,)),
        ],
        compiler_params=pltpu.CompilerParams(
            collective_id=0, has_side_effects=True, vmem_limit_bytes=38 * 2**20
        ),
        cost_estimate=pl.CostEstimate(flops=int(2e10), bytes_accessed=int(5e7), transcendentals=0),
        name="prepare",
    )(features.reshape(across, stride, piece, feat))


def schur_body(
    row_ref, col_ref, rows_ref, cols_ref, all_panels_ref, p_ref, q_ref, out_ref, panel_ref,
    panel_sem,
):
    own_row, own_col = row_ref[0], col_ref[0]
    row_count, col_count = lax.axis_size("row"), lax.axis_size("col")
    across, tile_len = cols_ref.shape[0], cols_ref.shape[1]
    stride = rows_ref.shape[1]
    chunks = across * tile_len // LEAF
    per = tile_len // LEAF
    g = pl.program_id(0)
    out_panels = pltpu.make_async_copy(all_panels_ref, panel_ref, panel_sem)

    @pl.when(g == 0)
    def _():
        out_panels.start()

    size = stride * tile_len
    here = pl.ds(pl.multiple_of(g * size, size), size)
    points = rows_ref[g].reshape(size, rows_ref.shape[3])
    p = p_ref[here, :]
    for b in range(across):
        less = dot(p, q_ref[b * tile_len:(b + 1) * tile_len, :], NT)
        s = gram(points, cols_ref[b]) - less
        for k in range(per):
            out_ref[pl.ds(b * per + k, size, stride=chunks), :] = s[:, k * LEAF:(k + 1) * LEAF]

    for turn in range(stride):
        tile_id = (g * stride + turn) * row_count + own_row
        for b in range(across):
            @pl.when(tile_id == b * col_count + own_col)
            def _():
                ident = eye(tile_len)
                for k in range(per):
                    at = pl.ds(turn * tile_len * chunks + b * per + k, tile_len, stride=chunks)
                    out_ref[at, :] = out_ref[at, :] + ident[:, k * LEAF:(k + 1) * LEAF]

    @pl.when(g == pl.num_programs(0) - 1)
    def _():
        out_panels.wait()


def schur(own_row, own_col, row_points, col_points, panels, p, q):
    across, stride, tile_len, _ = row_points.shape
    size = stride * tile_len
    chunks = across * tile_len // LEAF
    here = pl.BlockSpec(memory_space=pltpu.VMEM)
    scalar = pl.BlockSpec(memory_space=pltpu.SMEM)
    return pl.pallas_call(
        schur_body,
        out_shape=(
            jax.ShapeDtypeStruct((across * size * chunks, LEAF), F32),
            jax.ShapeDtypeStruct(panels.shape, F32),
        ),
        grid=(across,),
        in_specs=[scalar] * 2 + [here] * 5,
        out_specs=(
            pl.BlockSpec((size * chunks, LEAF), lambda g: (g, 0)),
            pl.BlockSpec(memory_space=pl.ANY),
        ),
        scratch_shapes=[pltpu.SemaphoreType.DMA],
        compiler_params=pltpu.CompilerParams(
            dimension_semantics=("arbitrary",), vmem_limit_bytes=28 * 2**20
        ),
        name="schur",
    )(own_row.reshape(1), own_col.reshape(1), row_points, col_points, panels, p, q)


def per_device(features):
    row_count = lax.axis_size("row")
    col_count = lax.axis_size("col")
    local_tiles, _, piece, feat = features.shape
    tile_len = piece * col_count
    rows, cols, tall_panels, p, q = prepare(features[:, 0], row_count, col_count)
    big, panels = schur(
        lax.axis_index("row"), lax.axis_index("col"), rows, cols, tall_panels, p, q
    )
    across = cols.shape[0]
    return (
        big.reshape(local_tiles, 1, tile_len, across, 1, tile_len),
        panels.reshape(local_tiles, 1, tile_len, 2 * tile_len),
    )


def solution(mesh):
    return jax.shard_map(
        per_device,
        mesh=mesh,
        in_specs=(P(None, "row", "col", None),),
        out_specs=(P(None, "row", None, None, "col", None), P(None, "row", None, None)),
        check_vma=False,
    )
```

```python
import math

import jax
import jax.numpy as jnp
from jax import lax
from jax.experimental import pallas as pl
from jax.experimental.pallas import tpu as pltpu
from jax.sharding import PartitionSpec as P

kernel_gain = 2.0
epsilon = 1e-06
LEAF = 128
SUB = 16
gain2 = kernel_gain / math.log(2.0)
BF = jnp.bfloat16
F32 = jnp.float32
NT = (((1,), (1,)), ((), ()))
NN = (((1,), (0,)), ((), ()))
TN = (((0,), (0,)), ((), ()))


def split(x):
    hi = x.astype(BF)
    return hi, (x - hi.astype(F32)).astype(BF)


def dot(a, b, dims):
    return lax.dot_general(a, b, dims, preferred_element_type=F32)


def dot3(a, b, dims):
    ah, al = a
    bh, bl = b
    return dot(ah, bh, dims) + (dot(ah, bl, dims) + dot(al, bh, dims))


def gram(a, b):
    return jnp.exp2(gain2 * dot(a, b, NT) - gain2)


def eye(n):
    return (
        lax.broadcasted_iota(jnp.int32, (n, n), 0) == lax.broadcasted_iota(jnp.int32, (n, n), 1)
    ).astype(F32)


def half_leaf(block, sides):
    size = block.shape[0]
    groups = size // SUB
    x = [[m[g * SUB:(g + 1) * SUB] for g in range(groups)] for m in (block, *sides)]
    sub = lax.broadcasted_iota(jnp.int32, (SUB, LEAF), 0)

    def lane(v, at):
        return jnp.broadcast_to(v[:, at:at + 1], (SUB, LEAF))

    def row(v, at):
        return jnp.broadcast_to(v[at:at + 1, :], v.shape)

    for p in range(groups):
        c = [lane(x[0][p], p * SUB + k) for k in range(SUB)]
        pairs = []
        for j in range(0, SUB, 2):
            a, e, f = row(c[j], j), row(c[j], j + 1), row(c[j + 1], j + 1)
            r1, rd = lax.rsqrt(a), lax.rsqrt(a * f - e * e)
            across = e * r1
            r2 = a * r1 * rd
            l1 = c[j] * r1
            l2 = (c[j + 1] - l1 * across) * r2
            u1 = {k: row(l1, k) for k in range(j + 2, SUB)}
            u2 = {k: row(l2, k) for k in range(j + 2, SUB)}
            for k in range(j + 2, SUB):
                c[k] = c[k] - l1 * u1[k] - l2 * u2[k]
            b1 = jnp.where(sub > j + 1, l1, 0.0)
            b2 = jnp.where(sub > j + 1, l2, 0.0)
            w = []
            for m in x:
                w1 = row(m[p], j) * r1
                w2 = (row(m[p], j + 1) - w1 * across) * r2
                m[p] = jnp.where(
                    sub == j, w1, jnp.where(sub == j + 1, w2, m[p] - b1 * w1 - b2 * w2)
                )
                w.append((w1, w2))
            pairs.append((j, r1, across, r2, u1, u2, w))
        for g in range(p + 1, groups):
            c = [lane(x[0][g], p * SUB + k) for k in range(SUB)]
            for j, r1, across, r2, u1, u2, w in pairs:
                l1 = c[j] * r1
                l2 = (c[j + 1] - l1 * across) * r2
                for k in range(j + 2, SUB):
                    c[k] = c[k] - l1 * u1[k] - l2 * u2[k]
                for m, (w1, w2) in zip(x, w):
                    m[g] = m[g] - l1 * w1 - l2 * w2
    return [jnp.concatenate(m, axis=0) for m in x]


def leaf(block, rest=None):
    h = LEAF // 2
    ident = eye(LEAF)
    upper, first = half_leaf(block[:h], [ident[:h]])
    right = jnp.where(lax.broadcasted_iota(jnp.int32, (h, LEAF), 1) >= h, upper, 0.0)
    rs = split(right)
    lower = block[h:] - dot3(rs, rs, TN)[h:]
    fs = split(first)
    cross = dot3(rs, fs, TN)[h:]
    if rest is not None:
        top = dot3(fs, split(rest), NN)
        pre = rest[h:] - dot3(rs, split(top), TN)[h:]
    packed = pltpu.roll(lower, h, 1)
    wide = lax.broadcasted_iota(jnp.int32, (h, LEAF), 1)
    packed = jnp.where(wide < h, packed, ident[:h][:, :])
    packed = jnp.where(wide < h, packed, pltpu.roll(ident[:h], h, 1))
    done = half_leaf(packed, [])[0]
    second = jnp.where(wide >= h, done, 0.0)
    inner = pltpu.roll(second, h, 1)
    inner = split(inner)
    low = second - dot3(inner, split(jnp.concatenate([cross, jnp.zeros_like(cross)], axis=0)), NN)
    inverse = jnp.concatenate([first, low], axis=0)
    if rest is None:
        return inverse, None
    bottom = dot3(inner, split(jnp.concatenate([pre, jnp.zeros_like(pre)], axis=0)), NN)
    return inverse, jnp.concatenate([top, bottom], axis=0)


def factor_steps(front, work, between):
    n = front.shape[0]
    blocks = n // LEAF
    spans = [slice(b * LEAF, (b + 1) * LEAF) for b in range(blocks)]
    m_spans = [slice(n + b * LEAF, n + (b + 1) * LEAF) for b in range(blocks)]
    for b in range(blocks):
        work[spans[b], b * LEAF:n] = gram(front[spans[b]], front[b * LEAF:])
    ident = eye(LEAF)
    block = work[spans[0], spans[0]] + ident
    for b in range(blocks):
        up = (b + 1) * LEAF
        inverse, right = leaf(block, work[spans[b], up:n] if up < n else None)
        inv = split(inverse)
        work[spans[b], m_spans[b]] = inverse
        if up < n:
            rs = split(right)
            rest = [tuple(v[:, i * LEAF:(i + 1) * LEAF] for v in rs) for i in range(blocks - b - 1)]
            block = work[spans[b + 1], spans[b + 1]] + ident - dot3(rest[0], rest[0], TN)
        between(b)
        if b:
            left = dot3(inv, split(work[spans[b], n:n + b * LEAF]), NN)
            work[spans[b], n:n + b * LEAF] = left
        if up < n:
            ms = split(work[spans[b], n:n + up])
            for i in range(b + 1, blocks):
                ri = rest[i - b - 1]
                at = i * LEAF
                if i > b + 1:
                    ahead = tuple(v[:, (i - b - 1) * LEAF:] for v in rs)
                    work[spans[i], at:n] = work[spans[i], at:n] - dot3(ri, ahead, TN)
                elif i + 1 < blocks:
                    ahead = tuple(v[:, LEAF:] for v in rs)
                    work[spans[i], at + LEAF:n] = work[spans[i], at + LEAF:n] - dot3(ri, ahead, TN)
                change = dot3(ri, ms, TN)
                if b:
                    old = slice(n, n + b * LEAF)
                    work[spans[i], old] = work[spans[i], old] - change[:, :b * LEAF]
                work[spans[i], m_spans[b]] = -change[:, b * LEAF:]
    for b in range(blocks):
        if b + 1 < blocks:
            work[spans[b], n + (b + 1) * LEAF:2 * n] = jnp.zeros((LEAF, n - (b + 1) * LEAF), F32)


def panel_steps(points, tile_id, front, hi_ref, lo_ref, keep):
    t = points.shape[0]
    values = gram(points, front)
    at = lax.broadcasted_iota(jnp.int32, values.shape, 0) + tile_id * t
    values = values + (at == lax.broadcasted_iota(jnp.int32, values.shape, 1)).astype(F32)
    hi, lo = split(values)
    yield
    first = dot3((hi[:, :t], lo[:, :t]), (hi_ref[:t, :t], lo_ref[:t, :t]), NT)
    yield
    second = dot3((hi, lo), (hi_ref[t:, :], lo_ref[t:, :]), NT)
    yield
    keep(first, second)
    yield


def together(steps):
    for _ in zip(*steps):
        pass


def prepare_body(
    features_ref, rows_ref, cols_ref, panel_ref, p_ref, q_ref, held, slips, front_ref, hi_ref,
    lo_ref, work, tall_send,
    tall_recv, slip_send, slip_recv, front_send, front_recv, row_send, row_recv, pass_send,
    pass_recv, col_send, col_recv, keep_sem,
):
    rows = lax.axis_size("row")
    peers = lax.axis_size("col")
    r = lax.axis_index("row")
    c = lax.axis_index("col")
    stride, piece = features_ref.shape[1], features_ref.shape[2]
    tile_len = piece * peers
    pairs = peers // 2
    partner = c + 1 - 2 * lax.rem(c, 2)

    def at_row(d):
        return lax.rem(r + d, rows), c

    def at_col(peer):
        return r, peer

    barrier = pltpu.get_barrier_semaphore()
    for d in range(1, rows):
        pl.semaphore_signal(
            barrier, inc=1, device_id=at_row(d), device_id_type=pl.DeviceIdType.MESH
        )
    for d in range(1, peers):
        pl.semaphore_signal(
            barrier, inc=1, device_id=at_col(lax.rem(c + d, peers)),
            device_id_type=pl.DeviceIdType.MESH,
        )

    floated = features_ref[...].astype(F32)
    total = jnp.sum(floated * floated, axis=-1, keepdims=True)
    held[r] = (floated * lax.rsqrt(total + epsilon)).astype(BF)
    pl.semaphore_wait(barrier, rows + peers - 2)

    def remote(src, dst, send, recv, target):
        return pltpu.make_async_remote_copy(
            src_ref=src, dst_ref=dst, send_sem=send, recv_sem=recv, device_id=target,
            device_id_type=pl.DeviceIdType.MESH,
        )

    def strip(peer):
        return pl.ds(pl.multiple_of(peer * piece, piece), piece)

    here = strip(c)

    def slip(tile, d, target):
        return remote(
            held.at[tile, 0, 0], slips.at[tile], slip_send.at[tile, d], slip_recv.at[tile], target
        )

    for tile in range(2):
        @pl.when(r == tile)
        def _():
            for d in range(1, rows):
                slip(tile, d, at_row(d)).start()
            own = pltpu.make_async_copy(held.at[tile, 0, 0], slips.at[tile], keep_sem.at[0])
            own.start()
            own.wait()

    def up(step, owner, target):
        return remote(
            held.at[owner], held.at[owner], tall_send.at[0, step], tall_recv.at[0, step],
            (target, c),
        )

    def down(step, owner, target):
        return remote(
            held.at[owner], held.at[owner], tall_send.at[1, step], tall_recv.at[1, step],
            (target, c),
        )

    def hop(step):
        @pl.when((r + 1 < rows) & (r - step >= 0))
        def _():
            up(step, r - step, r + 1).start()

        @pl.when((r - 1 >= 0) & (r + step < rows))
        def _():
            down(step, r + step, r - 1).start()

    hop(0)

    for tile in range(2):
        @pl.when(r != tile)
        def _():
            slip(tile, 1, at_row(1)).wait_recv()

    def front_copy(d, owner, target):
        return remote(
            slips, front_ref.at[:, strip(owner)], front_send.at[d], front_recv.at[d], target
        )

    for d in range(1, peers):
        front_copy(d, c, at_col(lax.rem(c + d, peers))).start()
    kept = [
        pltpu.make_async_copy(slips, front_ref.at[:, here], keep_sem.at[0]),
        pltpu.make_async_copy(held.at[r], rows_ref.at[:, :, here], keep_sem.at[1]),
    ]
    for copy in kept:
        copy.start()

    def row_copy(d, owner, target):
        return remote(
            held.at[r], rows_ref.at[:, :, strip(owner)], row_send.at[d], row_recv.at[d], target
        )

    def pass_copy(d, owner, target):
        there = rows_ref.at[:, :, strip(owner)]
        return remote(there, there, pass_send.at[d], pass_recv.at[d], target)


    def col_copy(block, turn, owner, target):
        away = lax.rem(target - owner + peers, peers)
        return remote(
            held.at[block, :, turn], cols_ref.at[:, strip(owner)], col_send.at[away],
            col_recv.at[away], at_col(target),
        )

    def hand_out(block):
        for turn in range(stride):
            peer = block + turn * rows

            @pl.when(peer != c)
            def _():
                col_copy(block, turn, c, peer).start()

            @pl.when(peer == c)
            def _():
                pltpu.make_async_copy(
                    held.at[block, :, turn], cols_ref.at[:, here], keep_sem.at[2]
                ).start()

    def arrive(step):
        @pl.when(r - 1 - step >= 0)
        def _():
            up(step, r - 1 - step, r - 1).wait_recv()

        @pl.when(r + 1 + step < rows)
        def _():
            down(step, r + 1 + step, r + 1).wait_recv()

        if step + 2 < rows:
            hop(step + 1)

    def share(step):
        @pl.when(r - 1 - step >= 0)
        def _():
            hand_out(r - 1 - step)

        @pl.when(r + 1 + step < rows)
        def _():
            hand_out(r + 1 + step)

    arrive(0)
    for d in range(1, peers):
        front_copy(d, lax.rem(c - d + peers, peers), at_col(c)).wait_recv()
    kept[0].wait()
    row_copy(0, c, at_col(partner)).start()
    for d in range(1, pairs):
        row_copy(d, c, at_col(lax.rem(c + 2 * d, peers))).start()
    share(0)

    def pass_on():
        for d in range(1, pairs):
            owner = lax.rem(c - 2 * d + peers, peers)
            row_copy(d, owner, at_col(partner)).wait_recv()
            pass_copy(d, owner, at_col(partner)).start()

    blocks = 2 * tile_len // LEAF

    def between(at):
        step = at // 2 + 1
        if at == blocks - 1:
            pass_on()
        if at % 2 and step < rows - 1:
            arrive(step)
            share(step)

    front = front_ref[...].reshape(2 * tile_len, front_ref.shape[2])
    factor_steps(front, work, between)
    n = front.shape[0]
    for step in range(blocks // 2 + 1, rows - 1):
        arrive(step)
        share(step)
    hi, lo = split(work[:, n:2 * n])
    hi_ref[...] = hi
    lo_ref[...] = lo

    kept[1].wait()
    row_copy(0, partner, at_col(partner)).wait_recv()
    row_copy(0, c, at_col(partner)).wait_send()
    for d in range(1, pairs):
        owner = lax.rem(partner - 2 * d + peers, peers)
        pass_copy(d, owner, at_col(partner)).wait_recv()
        pass_copy(d, lax.rem(c - 2 * d + peers, peers), at_col(partner)).wait_send()
        row_copy(d, c, at_col(partner)).wait_send()

    def one_row(at):
        def step(turn):
            tile = at * stride + turn
            here = pl.ds(pl.multiple_of(tile * tile_len, tile_len), tile_len)

            def keep(first, second):
                fh, fl = split(first)
                panel_ref[here, :tile_len] = first
                panel_ref[here, tile_len:] = second
                p_ref[here, :tile_len] = fh
                p_ref[here, tile_len:n] = second.astype(BF)
                p_ref[here, n:n + LEAF] = fh[:, :LEAF]
                p_ref[here, n + LEAF:] = fl[:, :LEAF]

            return panel_steps(
                rows_ref[at, turn], tile * rows + r, front, hi_ref, lo_ref, keep
            )

        return step

    def row_panels(at, carry):
        together(
            [one_row(at * deep + k)(turn) for k in range(deep) for turn in range(stride)]
        )
        return carry

    deep = math.gcd(rows_ref.shape[0], 6)
    lax.fori_loop(0, rows_ref.shape[0] // deep, row_panels, 0)

    for d in range(1, peers):
        front_copy(d, c, at_col(partner)).wait_send()

    own_cols = pltpu.make_async_copy(rows_ref.at[:, c // rows], cols_ref, keep_sem.at[2])

    @pl.when(lax.rem(c, rows) == r)
    def _():
        own_cols.start()
        own_cols.wait()

    @pl.when(lax.rem(c, rows) != r)
    def _():
        pltpu.make_async_copy(held.at[0, :, 0], cols_ref.at[:, here], keep_sem.at[2]).wait()
        for d in range(1, peers):
            col_copy(0, 0, lax.rem(c - d + peers, peers), c).wait_recv()

    def one_column(b):
        here = slice(b * tile_len, (b + 1) * tile_len)

        def keep(first, second):
            fh, fl = split(first)
            q_ref[here, :tile_len] = fh
            q_ref[here, tile_len:n] = second.astype(BF)
            q_ref[here, n:n + LEAF] = fl[:, :LEAF]
            q_ref[here, n + LEAF:] = fh[:, :LEAF]

        return panel_steps(cols_ref[b], b * peers + c, front, hi_ref, lo_ref, keep)

    together([one_column(b) for b in range(cols_ref.shape[0])])

    for d in range(1, peers):
        @pl.when(lax.rem(lax.rem(c + d, peers), rows) != r)
        def _():
            col_copy(0, 0, c, lax.rem(c + d, peers)).wait_send()
    for step in range(rows - 1):
        @pl.when((r + 1 < rows) & (r - step >= 0))
        def _():
            up(step, r, r + 1).wait_send()

        @pl.when((r - 1 >= 0) & (r + step < rows))
        def _():
            down(step, r, r - 1).wait_send()
    for tile in range(2):
        @pl.when(r == tile)
        def _():
            for d in range(1, rows):
                slip(tile, d, at_row(d)).wait_send()


def prepare(features, row_count, col_count):
    local_tiles, piece, feat = features.shape
    stride = col_count // row_count
    across = local_tiles // stride
    tile_len = piece * col_count
    n = 2 * tile_len
    dma = pltpu.SemaphoreType.DMA
    vmem = pl.BlockSpec(memory_space=pltpu.VMEM)
    rows = local_tiles * tile_len
    cols = across * tile_len
    return pl.pallas_call(
        prepare_body,
        out_shape=(
            jax.ShapeDtypeStruct((across, stride, tile_len, feat), BF),
            jax.ShapeDtypeStruct((across, tile_len, feat), BF),
            jax.ShapeDtypeStruct((rows, n), F32),
            jax.ShapeDtypeStruct((rows, n + 2 * LEAF), BF),
            jax.ShapeDtypeStruct((cols, n + 2 * LEAF), BF),
        ),
        in_specs=[vmem],
        out_specs=(vmem,) * 5,
        scratch_shapes=[
            pltpu.VMEM((row_count, across, stride, piece, feat), BF),
            pltpu.VMEM((2, piece, feat), BF),
            pltpu.VMEM((2, tile_len, feat), BF),
            pltpu.VMEM((n, n), BF),
            pltpu.VMEM((n, n), BF),
            pltpu.VMEM((n, 2 * n), F32),
            dma((2, row_count)), dma((2, row_count)), dma((2, row_count)), dma((2,)),
            dma((col_count,)), dma((col_count,)), dma((col_count,)), dma((col_count,)),
            dma((col_count,)), dma((col_count,)), dma((col_count,)), dma((col_count,)), dma((3,)),
        ],
        compiler_params=pltpu.CompilerParams(
            collective_id=0, has_side_effects=True, vmem_limit_bytes=38 * 2**20
        ),
        cost_estimate=pl.CostEstimate(flops=int(2e10), bytes_accessed=int(5e7), transcendentals=0),
        name="prepare",
    )(features.reshape(across, stride, piece, feat))


def schur_body(
    row_ref, col_ref, rows_ref, cols_ref, all_panels_ref, p_ref, q_ref, out_ref, panel_ref,
    panel_sem,
):
    own_row, own_col = row_ref[0], col_ref[0]
    row_count, col_count = lax.axis_size("row"), lax.axis_size("col")
    across, tile_len = cols_ref.shape[0], cols_ref.shape[1]
    stride = rows_ref.shape[1]
    chunks = across * tile_len // LEAF
    per = tile_len // LEAF
    g = pl.program_id(0)
    out_panels = pltpu.make_async_copy(all_panels_ref, panel_ref, panel_sem)

    @pl.when(g == 0)
    def _():
        out_panels.start()

    size = stride * tile_len
    here = pl.ds(pl.multiple_of(g * size, size), size)
    points = rows_ref[g].reshape(size, rows_ref.shape[3])
    p = p_ref[here, :]
    for b in range(across):
        less = dot(p, q_ref[b * tile_len:(b + 1) * tile_len, :], NT)
        s = gram(points, cols_ref[b]) - less
        for k in range(per):
            out_ref[pl.ds(b * per + k, size, stride=chunks), :] = s[:, k * LEAF:(k + 1) * LEAF]

    for turn in range(stride):
        tile_id = (g * stride + turn) * row_count + own_row
        for b in range(across):
            @pl.when(tile_id == b * col_count + own_col)
            def _():
                ident = eye(tile_len)
                for k in range(per):
                    at = pl.ds(turn * tile_len * chunks + b * per + k, tile_len, stride=chunks)
                    out_ref[at, :] = out_ref[at, :] + ident[:, k * LEAF:(k + 1) * LEAF]

    @pl.when(g == pl.num_programs(0) - 1)
    def _():
        out_panels.wait()


def schur(own_row, own_col, row_points, col_points, panels, p, q):
    across, stride, tile_len, _ = row_points.shape
    size = stride * tile_len
    chunks = across * tile_len // LEAF
    here = pl.BlockSpec(memory_space=pltpu.VMEM)
    scalar = pl.BlockSpec(memory_space=pltpu.SMEM)
    return pl.pallas_call(
        schur_body,
        out_shape=(
            jax.ShapeDtypeStruct((across * size * chunks, LEAF), F32),
            jax.ShapeDtypeStruct(panels.shape, F32),
        ),
        grid=(across,),
        in_specs=[scalar] * 2 + [here] * 5,
        out_specs=(
            pl.BlockSpec((size * chunks, LEAF), lambda g: (g, 0)),
            pl.BlockSpec(memory_space=pl.ANY),
        ),
        scratch_shapes=[pltpu.SemaphoreType.DMA],
        compiler_params=pltpu.CompilerParams(
            dimension_semantics=("arbitrary",), vmem_limit_bytes=28 * 2**20
        ),
        name="schur",
    )(own_row.reshape(1), own_col.reshape(1), row_points, col_points, panels, p, q)


def per_device(features):
    row_count = lax.axis_size("row")
    col_count = lax.axis_size("col")
    local_tiles, _, piece, feat = features.shape
    tile_len = piece * col_count
    rows, cols, tall_panels, p, q = prepare(features[:, 0], row_count, col_count)
    big, panels = schur(
        lax.axis_index("row"), lax.axis_index("col"), rows, cols, tall_panels, p, q
    )
    across = cols.shape[0]
    return (
        big.reshape(local_tiles, 1, tile_len, across, 1, tile_len),
        panels.reshape(local_tiles, 1, tile_len, 2 * tile_len),
    )


def solution(mesh):
    return jax.shard_map(
        per_device,
        mesh=mesh,
        in_specs=(P(None, "row", "col", None),),
        out_specs=(P(None, "row", None, None, "col", None), P(None, "row", None, None)),
        check_vma=False,
    )
```
